128 devices in a mesh: gx: 8 (over z, core), gy: 4 (over x), gz: 4 (over y).
Axes of the slice: x: 4, y: 4, z: 4, core: 2. Of those that a mesh axis runs over, the one named last changes fastest.
Arguments:
- snapshots: float32 [16, 128, 128, 1024], P(None, 'gx', 'gy', 'gz'), as said below
- diffusivity: float32 [128, 128, 1024], P('gx', 'gy', 'gz'), may hold values from 0.02 to 0.16
Outputs:
- shifted: float32 [16, 128, 128, 1024], P(None, 'gx', 'gy', 'gz')
- reduced: float32 [16, 16], replicated
- sigmas: float32 [16], replicated
The draws below stay inside these ranges and needn't reach their ends.
Inputs may be any that keep to these rules, and one draw needn't show every extreme that they name: `snapshots`: real values.
All inputs are finite; a program needn't handle non-finite values.
Results may differ from the reference program's by a relative error of at most 0.0003.
Values sent between devices are 32-bit elements; how exact they have to be, the bound alone decides.
A program may use at most 128 MiB of HBM per device.

```python
import math
import jax
import jax.numpy as jnp
import numpy as np
from jax import lax

SNAPS = 16
RANK = 12
SWEEPS = 6
NX = 128
NY = 128
NZ = 1024


def draw_snapshots(key, part):
    key_noise, key_mix = jax.random.split(jax.random.fold_in(key, 17))
    shape = (SNAPS, NX, NY, NZ)
    noise = jnp.clip(jax.random.normal(key_noise, shape, jnp.float32), -6.0, 6.0)
    slope = 2.0
    for axis_pos in (1, 2, 3):
        noise = (noise + jnp.roll(noise, 1, axis=axis_pos)) * 0.70710678
    reflect = jax.random.normal(key_mix, (SNAPS, SNAPS), jnp.float32)
    rotation = jnp.eye(SNAPS, dtype=jnp.float32)
    for reflect_pos in range(SNAPS):
        vector = reflect[reflect_pos]
        image = jnp.dot(rotation, vector, precision=lax.Precision.HIGHEST)
        rotation = rotation - 2.0 / jnp.sum(vector * vector) * (image[:, None] * vector[None, :])
    index = jnp.arange(SNAPS).astype(jnp.float32)
    scales = jnp.where(index < RANK, 3.0 * 0.9 ** index, 0.3 * 0.8 ** (index - RANK))
    mixing = rotation * scales[None, :]
    fields = jnp.einsum('kj,jxyz->kxyz', mixing, noise, precision=lax.Precision.HIGHEST)
    envelope = 1.0 + slope * jnp.arange(NX).astype(jnp.float32) / max(NX - 1, 1)
    return fields * envelope[None, :, None, None]


def steps_of(own_key, dims, cuts, least, largest):
    def one(axis_at, shards_of):
        heights = jax.random.uniform(jax.random.fold_in(jax.random.fold_in(own_key, 6), axis_at), (shards_of,), jnp.float32, least / len(cuts), largest / len(cuts))
        return jnp.repeat(jnp.exp(heights), dims[axis_at] // shards_of).reshape((-1,) + (1,) * (len(dims) - axis_at - 1))

    gain = one(*cuts[0])
    for cut in cuts[1:]:
        gain = gain * one(*cut)
    return gain


def setup_inputs(seed: int = 0) -> dict:
    splits = jax.random.split(jax.random.key(seed), 3)
    return {
        "snapshots": draw_snapshots(jax.random.fold_in(splits[2], 71), 0),
        "diffusivity": jnp.clip(jnp.exp(math.log(0.16) - 2.0794415 * jax.random.uniform(splits[1], (NX, NY, NZ), jnp.float32) ** steps_of(splits[1], (NX, NY, NZ), ((0, 8), (1, 4), (2, 4)), -0.2, 0.2)), 0.02, 0.16),
    }


def round_pairs(count):
    players = list(range(count))
    firsts = []
    seconds = []
    for turn in range(count - 1):
        firsts.append([players[i] for i in range(count // 2)])
        seconds.append([players[count - 1 - i] for i in range(count // 2)])
        players = [players[0]] + [players[-1]] + players[1:-1]
    return (np.array(firsts, dtype=np.int32), np.array(seconds, dtype=np.int32))

def jacobi_eigen(small):
    count = small.shape[0]
    first_np, second_np = round_pairs(count)
    firsts = jnp.asarray(first_np)
    seconds = jnp.asarray(second_np)
    eye = jnp.eye(count, dtype=jnp.float32)
    high = lax.Precision.HIGHEST

    def turn(step, carry):
        mat, vecs = carry
        row = step % (count - 1)
        pidx = firsts[row]
        qidx = seconds[row]
        app = mat[pidx, pidx]
        aqq = mat[qidx, qidx]
        apq = mat[pidx, qidx]
        tau = aqq - app
        sgn = jnp.where(tau >= 0, 1.0, -1.0).astype(jnp.float32)
        denom = jnp.abs(tau) + jnp.sqrt(tau * tau + 4.0 * apq * apq)
        tangent = jnp.where(denom > 0, 2.0 * apq * sgn / jnp.where(denom > 0, denom, 1.0), 0.0)
        cosine = 1.0 / jnp.sqrt(1.0 + tangent * tangent)
        sine = tangent * cosine
        onep = jax.nn.one_hot(pidx, count, dtype=jnp.float32)
        oneq = jax.nn.one_hot(qidx, count, dtype=jnp.float32)
        rot = eye + jnp.dot(onep.T, (cosine - 1.0)[:, None] * onep, precision=high)
        rot = rot + jnp.dot(oneq.T, (cosine - 1.0)[:, None] * oneq, precision=high)
        rot = rot + jnp.dot(onep.T, sine[:, None] * oneq, precision=high)
        rot = rot - jnp.dot(oneq.T, sine[:, None] * onep, precision=high)
        mat = jnp.dot(jnp.dot(rot.T, mat, precision=high), rot, precision=high)
        vecs = jnp.dot(vecs, rot, precision=high)
        return (mat, vecs)
    mat, vecs = lax.fori_loop(0, SWEEPS * (count - 1), turn, (small, eye))
    return (jnp.diagonal(mat), vecs)

def factor_pair(gram, cross):
    lower = jnp.linalg.cholesky(gram)
    proj = lax.linalg.triangular_solve(lower, cross, left_side=True, lower=True)
    return (lower.T, proj)

def finish(upper, proj, ncell):
    high = lax.Precision.HIGHEST
    small = jnp.dot(upper, upper.T, precision=high) / ncell
    lam, vecs = jacobi_eigen(small)
    ordered = jnp.sort(lam)[::-1]
    sigmas = jnp.sqrt(ordered)
    keep = (lam >= ordered[RANK - 1]).astype(jnp.float32)
    projector = jnp.dot(vecs * keep[None, :], vecs.T, precision=high)
    inverse = jnp.dot(vecs * (keep / lam)[None, :], vecs.T, precision=high) / ncell
    reduced = jnp.dot(jnp.dot(projector, proj, precision=high), upper.T, precision=high)
    reduced = jnp.dot(reduced, inverse, precision=high)
    return (reduced, sigmas)

def advance_field(field, diffusivity):

    def near(offset, dim):
        return jnp.roll(field, -offset, axis=dim)
    lap = -6.0 * field
    for dim in range(3):
        lap = lap + near(1, dim) + near(-1, dim)

    def slope(dim):
        return (8.0 * (near(1, dim) - near(-1, dim)) - (near(2, dim) - near(-2, dim))) / 12.0
    return field + diffusivity * lap - (0.3 + 0.02 * field) * slope(2) - 0.2 * slope(0) - 0.15 * slope(1)

def reference(snapshots, diffusivity):
    high = lax.Precision.HIGHEST
    shifted = lax.map(lambda field: advance_field(field, diffusivity), snapshots)
    flat_x = snapshots.reshape(SNAPS, -1)
    flat_y = shifted.reshape(SNAPS, -1)
    gram = jnp.dot(flat_x, flat_x.T, precision=high)
    cross = jnp.dot(flat_x, flat_y.T, precision=high)
    upper, proj = factor_pair(gram, cross)
    reduced, sigmas = finish(upper, proj, float(NX * NY * NZ))
    return (shifted, reduced, sigmas)
```

```python
import functools

import jax
import jax.numpy as jnp
from jax import lax
from jax.experimental import pallas as pl
from jax.experimental.pallas import tpu as pltpu
from jax.sharding import PartitionSpec as P

SNAPS = 16
RANK = 12
SWEEPS = 6
HIGH = lax.Precision.HIGHEST
F32 = jnp.float32
BF16 = jnp.bfloat16
MESH = pl.DeviceIdType.MESH
AXES = ("gx", "gy", "gz")


def peers(sizes):
    found = []
    for axis, count in zip(AXES, sizes):
        for step in range(1, count):
            found.append((axis, step, lax.rem(lax.axis_index(axis) + step, count)))
    return found


def enter(sizes):
    barrier = pltpu.get_barrier_semaphore()
    known = peers(sizes)
    for axis, _, target in known:
        pl.semaphore_signal(barrier, inc=1, device_id={axis: target}, device_id_type=MESH)
    pl.semaphore_wait(barrier, len(known))


def pack_square(square):
    return jnp.concatenate([square[0:8], square[8:16]], axis=1)


def unpack_square(packed):
    return jnp.concatenate([packed[:, 0:16], packed[:, 16:32]], axis=0)


def sum_over_mesh(sizes, value, slots, send_sems, recv_sems):
    at = 0
    for place, (axis, count) in enumerate(zip(AXES, sizes)):
        me = lax.axis_index(axis)
        base = 8 * place
        slots[base + me, :, 0:32] = value
        copies = []
        for step in range(1, count):
            target = lax.rem(me + step, count)
            copy = pltpu.make_async_remote_copy(
                src_ref=slots.at[base + me],
                dst_ref=slots.at[base + me],
                send_sem=send_sems.at[at],
                recv_sem=recv_sems.at[at],
                device_id={axis: target},
                device_id_type=MESH,
            )
            copy.start()
            copies.append(copy)
            at += 1
        for copy in copies:
            copy.wait()
        value = slots[base, :, 0:32]
        for slot in range(1, count):
            value = value + slots[base + slot, :, 0:32]
    return value


def halves(block):
    high = block.astype(BF16)
    return high, (block - high.astype(F32)).astype(BF16)


def fold(total, groups):
    sub = lax.broadcasted_iota(jnp.int32, (8, 256), 0)
    lane = lax.broadcasted_iota(jnp.int32, (8, 256), 1)
    same = (sub == lane % 8).astype(F32)
    rows = jnp.sum(total.reshape(groups * 16, 8, 256) * same[None], axis=1)
    pick = (
        lax.broadcasted_iota(jnp.int32, (256, 32), 0) // 8
        == lax.broadcasted_iota(jnp.int32, (256, 32), 1)
    ).astype(F32)
    return jnp.dot(rows, pick, precision=HIGH, preferred_element_type=F32)


NT = (((1,), (1,)), ((), ()))
TN = (((0,), (0,)), ((), ()))


def exchange_kernel(
    sizes, snap, xlo, xhi, ylo, yhi, zlo, zhi, gram,
    field, yplo, yphi, zplo, zphi, total, slots,
    load_sem, xs, xr, ys, yr, zs, zr, gs, gr,
):
    planes = field.shape[0]
    parts = 4
    each = planes // parts
    for x in range(planes):
        pltpu.make_async_copy(snap.at[:, x], field.at[x], load_sem.at[x]).start()
    enter(sizes)
    near = {}
    for axis, count in zip(AXES, sizes):
        me = lax.axis_index(axis)
        near[axis] = (lax.rem(me + count - 1, count), lax.rem(me + 1, count))

    def remote(src, dst, send, recv, axis, side):
        copy = pltpu.make_async_remote_copy(
            src_ref=src, dst_ref=dst, send_sem=send, recv_sem=recv,
            device_id={axis: near[axis][side]}, device_id_type=MESH,
        )
        copy.start()
        return copy

    copies = [
        remote(snap.at[:, 0:2], xhi, xs.at[0], xr.at[0], "gx", 0),
        remote(snap.at[:, planes - 2:planes], xlo, xs.at[1], xr.at[1], "gx", 1),
    ]
    lane = lax.broadcasted_iota(jnp.int32, (32, 128), 1)

    def plane(x, carry):
        pltpu.make_async_copy(snap.at[:, x], field.at[x], load_sem.at[x]).wait()
        left = jnp.zeros((32, 128), F32)
        right = jnp.zeros((32, 128), F32)
        for k in range(SNAPS):
            yplo[x, 2 * k:2 * k + 2, :] = field[x, k, 0:2, :]
            yphi[x, 2 * k:2 * k + 2, :] = field[x, k, 30:32, :]
            head = field[x, k, :, 0:128]
            tail = field[x, k, :, 128:256]
            if k:
                head = pltpu.roll(head, 8 * k, 1)
                tail = pltpu.roll(tail, 8 * k, 1)
            left = jnp.where((lane >= 8 * k) & (lane < 8 * k + 2), head, left)
            low = (8 * k - 2) % 128
            right = jnp.where((lane >= low) & (lane < low + 2), tail, right)
        zplo[x] = left
        zphi[x] = right
        return carry

    def inner(x, carry):
        highs, lows = [], []
        for a in range(4):
            high, low = halves(field[x, :, 8 * a:8 * a + 8, :].reshape(128, 256))
            highs.append(high)
            lows.append(low)
        high = jnp.concatenate(highs, axis=1)
        both = jnp.concatenate([high, jnp.concatenate(lows, axis=1)], axis=0)
        total[...] += lax.dot_general(both, both, NT, preferred_element_type=F32)
        return carry

    total[...] = jnp.zeros_like(total)
    for part in range(parts):
        span = pl.ds(part * each, each)
        lax.fori_loop(part * each, (part + 1) * each, plane, 0)
        copies += [
            remote(yplo.at[span], yhi.at[span], ys.at[2 * part], yr.at[2 * part], "gy", 0),
            remote(yphi.at[span], ylo.at[span], ys.at[2 * part + 1], yr.at[2 * part + 1], "gy", 1),
            remote(zplo.at[span], zhi.at[span], zs.at[2 * part], zr.at[2 * part], "gz", 0),
            remote(zphi.at[span], zlo.at[span], zs.at[2 * part + 1], zr.at[2 * part + 1], "gz", 1),
        ]
    lax.fori_loop(0, planes, inner, 0)
    small = fold(total[...], 2)
    mine = (small[0:16, 0:16] + small[16:32, 16:32]) + (small[0:16, 16:32] + small[16:32, 0:16])
    gram[...] = unpack_square(sum_over_mesh(sizes, pack_square(mine), slots, gs, gr))
    for copy in copies:
        copy.wait()


def factor(gram):
    row = lax.broadcasted_iota(jnp.int32, (16, 32), 0)
    col = lax.broadcasted_iota(jnp.int32, (16, 32), 1)
    mat = jnp.concatenate([gram, (row == col).astype(F32)[:, 0:16]], axis=1)
    for j in range(16):
        scale = lax.rsqrt(mat[j:j + 1, j:j + 1])
        top = mat[j:j + 1, :] * scale
        side = jnp.where(row[:, 0:1] > j, mat[:, j:j + 1] * scale, 0.0)
        mat = jnp.where(row == j, top, mat - side * top)
    upper = jnp.where(col[:, 0:16] >= row[:, 0:16], mat[:, 0:16], 0.0)
    return upper, mat[:, 16:32]


def jacobi_round(first, second):
    lane = lax.broadcasted_iota(jnp.int32, (8, 32), 1)
    sub = lax.broadcasted_iota(jnp.int32, (8, 32), 0)
    inside = lane < 16
    masked_first = jnp.where(inside, first, 0.0)
    masked_second = jnp.where(inside, second, 0.0)
    app = jnp.sum(masked_first * first, axis=1, keepdims=True)
    aqq = jnp.sum(masked_second * second, axis=1, keepdims=True)
    apq = jnp.sum(masked_first * second, axis=1, keepdims=True)
    tau = aqq - app
    square = tau * tau + 4.0 * apq * apq
    live = square > 0
    inverse = lax.rsqrt(jnp.where(live, square, 1.0))
    cos2 = 0.5 + 0.5 * jnp.abs(tau) * inverse
    root = lax.rsqrt(cos2)
    cosine = jnp.where(live, cos2 * root, 1.0)
    signed = jnp.where(tau >= 0, apq, -apq)
    sine = jnp.where(live, signed * inverse * root, 0.0)
    new_first = cosine * first - sine * second
    new_second = sine * first + cosine * second
    down = pltpu.roll(new_first, 1, 0)
    up = pltpu.roll(new_second, 7, 0)
    entering = pltpu.roll(new_second, 1, 0)
    top = jnp.where(sub == 0, new_first, jnp.where(sub == 1, entering, down))
    bottom = jnp.where(sub == 7, new_first, up)
    return top, bottom


def jacobi_start(upper):
    eye = (
        lax.broadcasted_iota(jnp.int32, (16, 16), 0) == lax.broadcasted_iota(jnp.int32, (16, 16), 1)
    ).astype(F32)
    both = jnp.concatenate([upper, eye], axis=1)
    return both[0:8], jnp.concatenate([both[i:i + 1] for i in range(15, 7, -1)], axis=0)


def spectrum(first, second, norm, ncell, upper, lower_inverse):
    both = jnp.concatenate([first, second], axis=0)
    scaled = both[:, 0:16]
    vecs = both[:, 16:32]
    lam = jnp.sum(scaled * scaled, axis=1, keepdims=True)
    row = lax.broadcasted_iota(jnp.int32, (16, 16), 0)
    col = lax.broadcasted_iota(jnp.int32, (16, 16), 1)
    along = jnp.sum(jnp.where(row == col, lam, 0.0), axis=0, keepdims=True)
    above = (along > lam).astype(F32)
    ties = ((along == lam) & (col < row)).astype(F32)
    greater = jnp.sum(above, axis=1, keepdims=True)
    keep = (greater < RANK - 0.5).astype(F32)
    place = greater + jnp.sum(ties, axis=1, keepdims=True)
    sigma = jnp.sqrt(lam * (norm / ncell))
    sigmas = jnp.sum(jnp.where(place == col.astype(F32), sigma, 0.0), axis=0, keepdims=True)
    proj = lax.dot_general(vecs * keep, vecs, TN, precision=HIGH, preferred_element_type=F32)
    weights = keep / (lam * norm)
    inverse = lax.dot_general(vecs * weights, vecs, TN, precision=HIGH, preferred_element_type=F32)
    before = jnp.dot(proj, lower_inverse, precision=HIGH, preferred_element_type=F32)
    after = lax.dot_general(upper, inverse, TN, precision=HIGH, preferred_element_type=F32)
    return before, after, sigmas


def shift_kernel(
    ncell, snap, diff, xlo, xhi, ylo, yhi, zlo, zhi, gram,
    out, crossing, before, after, sigmas,
    field, total, sems,
):
    x = pl.program_id(0)
    planes = pl.num_programs(0)
    static_planes = field.shape[0] - 4

    def load(p, half):
        lanes = pl.ds(half * 128, 128)
        return pltpu.make_async_copy(
            snap.at[:, p, :, lanes], field.at[p + 2, :, half, pl.ds(8, 32)], sems.at[p + 2, half]
        )

    def edge(side, p, half):
        lanes = pl.ds(half * 128, 128)
        source = (xlo, xhi)[side]
        slot = p if side == 0 else static_planes + 2 + p
        return pltpu.make_async_copy(
            source.at[:, p, :, lanes], field.at[slot, :, half, pl.ds(8, 32)], sems.at[slot, half]
        )

    @pl.when(x == 0)
    def _():
        total[...] = jnp.zeros_like(total)
        for half in range(2):
            for p in range(2):
                edge(0, p, half).start()
        for p in range(static_planes):
            for half in range(2):
                load(p, half).start()
        for half in range(2):
            for p in range(2):
                edge(1, p, half).start()
        for half in range(2):
            for p in range(2):
                edge(0, p, half).wait()
                load(p, half).wait()

    @pl.when(x < planes - 2)
    def _():
        for half in range(2):
            load(x + 2, half).wait()

    @pl.when(x >= planes - 2)
    def _():
        for half in range(2):
            edge(1, x - (planes - 2), half).wait()

    lane = lax.broadcasted_iota(jnp.int32, (32, 128), 1)
    group = lane % 8
    side = jnp.where(group < 4, zhi[0], zlo[0])
    for k in range(SNAPS):
        for half in range(2):
            lanes = pl.ds(half * 128, 128)
            field[x + 2, k, half, 6:8, :] = ylo[0, 2 * k:2 * k + 2, lanes]
            field[x + 2, k, half, 40:42, :] = yhi[0, 2 * k:2 * k + 2, lanes]

    def one(k, carry):
        base = 128 - 8 * k
        centre = [field[x + 2, k, half, 8:40, :] for half in range(2)]

        def moved(by):
            rolled = [pltpu.roll(c, by % 128, 1) for c in centre]
            outer = pltpu.roll(side, base + by, 1)
            if by > 0:
                return [
                    jnp.where(lane < by, outer, rolled[0]),
                    jnp.where(lane < by, rolled[0], rolled[1]),
                ]
            return [
                jnp.where(lane >= 128 + by, rolled[1], rolled[0]),
                jnp.where(lane >= 128 + by, outer, rolled[1]),
            ]

        zm1, zm2, zp1, zp2 = moved(1), moved(2), moved(-1), moved(-2)
        for half in range(2):
            u = centre[half]

            def at(dx, dy):
                return field[x + 2 + dx, k, half, 8 + dy:40 + dy, :]

            xp, xm, yp, ym = at(1, 0), at(-1, 0), at(0, 1), at(0, -1)
            zp, zm = zp1[half], zm1[half]
            lap = ((xp + xm) + (yp + ym)) + ((zp + zm) - 6.0 * u)
            flat = (8.0 / 12.0) * (0.2 * (xp - xm) + 0.15 * (yp - ym)) - (1.0 / 12.0) * (
                0.2 * (at(2, 0) - at(-2, 0)) + 0.15 * (at(0, 2) - at(0, -2))
            )
            steep = 8.0 * (zp - zm) - (zp2[half] - zm2[half])
            d = diff[0, :, half * 128:half * 128 + 128]
            new = u + d * lap - (0.3 / 12.0 + (0.02 / 12.0) * u) * steep - flat
            out[k, 0, :, half * 128:half * 128 + 128] = new
        return carry

    lax.fori_loop(0, SNAPS, one, 0)

    xh, xl, yh, yl = [], [], [], []
    for a in range(4):
        for half in range(2):
            high, low = halves(
                field[x + 2, :, half, 8 + 8 * a:16 + 8 * a, :].reshape(128, 128)
            )
            xh.append(high)
            xl.append(low)
            high, low = halves(
                out[:, 0, 8 * a:8 * a + 8, half * 128:half * 128 + 128].reshape(128, 128)
            )
            yh.append(high)
            yl.append(low)
    cat = functools.partial(jnp.concatenate, axis=1)
    total[...] += lax.dot_general(
        jnp.concatenate([cat(yh), cat(yl)], axis=0),
        jnp.concatenate([cat(xh), cat(xl)], axis=0),
        NT, preferred_element_type=F32,
    )

    @pl.when(x == planes - 1)
    def _():
        small = fold(total[...], 2)
        turned = (small[0:16, 0:16] + small[0:16, 16:32]) + (small[16:32, 0:16] + small[16:32, 16:32])
        crossing[...] = pack_square(turned)
        upper, lower_inverse = factor(gram[...])
        norm = jnp.sum(jnp.sum(upper * upper, axis=1, keepdims=True), axis=0, keepdims=True)
        first, second = jacobi_start(upper * lax.rsqrt(norm))

        def turn(step, pair):
            return jacobi_round(*pair)

        first, second = lax.fori_loop(0, SWEEPS * 15, turn, (first, second))
        before[...], after[...], sigmas[...] = spectrum(
            first, second, norm, ncell, upper, lower_inverse
        )


def finish_kernel(sizes, crossing, before, after, reduced, slots, gs, gr):
    enter(sizes)
    turned = unpack_square(sum_over_mesh(sizes, crossing[...], slots, gs, gr))
    inner = lax.dot_general(before[...], turned, NT, precision=HIGH, preferred_element_type=F32)
    reduced[...] = jnp.dot(inner, after[...], precision=HIGH, preferred_element_type=F32)


def shards(sizes, snapshots, diffusivity):
    planes = snapshots.shape[1]
    ncell = float(planes * 32 * 256 * sizes[0] * sizes[1] * sizes[2])
    hbm = pl.BlockSpec(memory_space=pl.ANY)
    vmem = pl.BlockSpec(memory_space=pltpu.VMEM)
    links = sum(count - 1 for count in sizes)
    dma = pltpu.SemaphoreType.DMA
    shape = functools.partial(jax.ShapeDtypeStruct, dtype=F32)
    *halos, gram = pl.pallas_call(
        functools.partial(exchange_kernel, sizes),
        name="exchange",
        out_shape=[
            shape((SNAPS, 2, 32, 256)), shape((SNAPS, 2, 32, 256)),
            shape((planes, 32, 256)), shape((planes, 32, 256)),
            shape((planes, 32, 128)), shape((planes, 32, 128)),
            shape((16, 16)),
        ],
        in_specs=[hbm],
        out_specs=[hbm] * 6 + [vmem],
        scratch_shapes=[
            pltpu.VMEM((planes, SNAPS, 32, 256), F32),
            pltpu.VMEM((planes, 32, 256), F32), pltpu.VMEM((planes, 32, 256), F32),
            pltpu.VMEM((planes, 32, 128), F32), pltpu.VMEM((planes, 32, 128), F32),
            pltpu.VMEM((256, 256), F32), pltpu.VMEM((24, 8, 128), F32),
            dma((planes,)), dma((2,)), dma((2,)), dma((8,)), dma((8,)), dma((8,)), dma((8,)),
            dma((links,)), dma((links,)),
        ],
        compiler_params=pltpu.CompilerParams(
            collective_id=0, has_side_effects=True, vmem_limit_bytes=40 << 20
        ),
    )(snapshots)
    row = lambda *block: pl.BlockSpec((1,) + block, lambda i: (i,) + (0,) * len(block))
    whole = lambda *block: pl.BlockSpec(block, lambda i: (0,) * len(block))
    shifted, crossing, before, after, sigmas = pl.pallas_call(
        functools.partial(shift_kernel, ncell),
        name="shift",
        grid=(planes,),
        out_shape=[
            shape(snapshots.shape), shape((8, 32)), shape((16, 16)), shape((16, 16)), shape((1, 16)),
        ],
        in_specs=[
            hbm, row(32, 256), hbm, hbm, row(32, 256), row(32, 256), row(32, 128), row(32, 128),
            whole(16, 16),
        ],
        out_specs=[
            pl.BlockSpec((SNAPS, 1, 32, 256), lambda i: (0, i, 0, 0)),
            whole(8, 32), whole(16, 16), whole(16, 16), whole(1, 16),
        ],
        scratch_shapes=[
            pltpu.VMEM((planes + 4, SNAPS, 2, 48, 128), F32),
            pltpu.VMEM((256, 256), F32),
            dma((planes + 4, 2)),
        ],
        compiler_params=pltpu.CompilerParams(vmem_limit_bytes=48 << 20),
    )(snapshots, diffusivity, *halos, gram)
    reduced = pl.pallas_call(
        functools.partial(finish_kernel, sizes),
        name="finish",
        out_shape=shape((16, 16)),
        in_specs=[vmem] * 3,
        out_specs=vmem,
        scratch_shapes=[pltpu.VMEM((24, 8, 128), F32), dma((links,)), dma((links,))],
        compiler_params=pltpu.CompilerParams(collective_id=1, has_side_effects=True),
    )(crossing, before, after)
    return (shifted, reduced, sigmas.reshape(16))


def solution(mesh):
    sizes = tuple(mesh.shape[axis] for axis in AXES)
    return jax.shard_map(
        functools.partial(shards, sizes),
        mesh=mesh,
        in_specs=(P(None, "gx", "gy", "gz"), P("gx", "gy", "gz")),
        out_specs=(P(None, "gx", "gy", "gz"), P(), P()),
        check_vma=False,
    )
```

```python
import functools

import jax
import jax.numpy as jnp
from jax import lax
from jax.experimental import pallas as pl
from jax.experimental.pallas import tpu as pltpu
from jax.sharding import PartitionSpec as P

SNAPS = 16
RANK = 12
SWEEPS = 6
HIGH = lax.Precision.HIGHEST
F32 = jnp.float32
BF16 = jnp.bfloat16
MESH = pl.DeviceIdType.MESH
AXES = ("gx", "gy", "gz")


def peers(sizes):
    found = []
    for axis, count in zip(AXES, sizes):
        for step in range(1, count):
            found.append((axis, step, lax.rem(lax.axis_index(axis) + step, count)))
    return found


def enter(sizes):
    barrier = pltpu.get_barrier_semaphore()
    known = peers(sizes)
    for axis, _, target in known:
        pl.semaphore_signal(barrier, inc=1, device_id={axis: target}, device_id_type=MESH)
    pl.semaphore_wait(barrier, len(known))


def pack_square(square):
    return jnp.concatenate([square[0:8], square[8:16]], axis=1)


def unpack_square(packed):
    return jnp.concatenate([packed[:, 0:16], packed[:, 16:32]], axis=0)


def sum_over_mesh(sizes, value, slots, send_sems, recv_sems):
    at = 0
    for place, (axis, count) in enumerate(zip(AXES, sizes)):
        me = lax.axis_index(axis)
        base = 8 * place
        slots[base + me, :, 0:32] = value
        copies = []
        for step in range(1, count):
            target = lax.rem(me + step, count)
            copy = pltpu.make_async_remote_copy(
                src_ref=slots.at[base + me],
                dst_ref=slots.at[base + me],
                send_sem=send_sems.at[at],
                recv_sem=recv_sems.at[at],
                device_id={axis: target},
                device_id_type=MESH,
            )
            copy.start()
            copies.append(copy)
            at += 1
        for copy in copies:
            copy.wait()
        value = slots[base, :, 0:32]
        for slot in range(1, count):
            value = value + slots[base + slot, :, 0:32]
    return value


def halves(block):
    high = block.astype(BF16)
    return high, (block - high.astype(F32)).astype(BF16)


def fold(total, groups):
    sub = lax.broadcasted_iota(jnp.int32, (8, 256), 0)
    lane = lax.broadcasted_iota(jnp.int32, (8, 256), 1)
    same = (sub == lane % 8).astype(F32)
    rows = jnp.sum(total.reshape(groups * 16, 8, 256) * same[None], axis=1)
    pick = (
        lax.broadcasted_iota(jnp.int32, (256, 32), 0) // 8
        == lax.broadcasted_iota(jnp.int32, (256, 32), 1)
    ).astype(F32)
    return jnp.dot(rows, pick, precision=HIGH, preferred_element_type=F32)


NT = (((1,), (1,)), ((), ()))
TN = (((0,), (0,)), ((), ()))


def exchange_kernel(
    sizes, snap, xlo, xhi, ylo, yhi, zlo, zhi, gram,
    field, yplo, yphi, zplo, zphi, total, slots,
    load_sem, xs, xr, ys, yr, zs, zr, gs, gr,
):
    planes = field.shape[0]
    parts = 4
    each = planes // parts
    for x in range(planes):
        pltpu.make_async_copy(snap.at[:, x], field.at[x], load_sem.at[x]).start()
    enter(sizes)
    near = {}
    for axis, count in zip(AXES, sizes):
        me = lax.axis_index(axis)
        near[axis] = (lax.rem(me + count - 1, count), lax.rem(me + 1, count))

    def remote(src, dst, send, recv, axis, side):
        copy = pltpu.make_async_remote_copy(
            src_ref=src, dst_ref=dst, send_sem=send, recv_sem=recv,
            device_id={axis: near[axis][side]}, device_id_type=MESH,
        )
        copy.start()
        return copy

    copies = [
        remote(snap.at[:, 0:2], xhi, xs.at[0], xr.at[0], "gx", 0),
        remote(snap.at[:, planes - 2:planes], xlo, xs.at[1], xr.at[1], "gx", 1),
    ]
    lane = lax.broadcasted_iota(jnp.int32, (32, 128), 1)

    def plane(x, carry):
        pltpu.make_async_copy(snap.at[:, x], field.at[x], load_sem.at[x]).wait()
        left = jnp.zeros((32, 128), F32)
        right = jnp.zeros((32, 128), F32)
        for k in range(SNAPS):
            yplo[x, 2 * k:2 * k + 2, :] = field[x, k, 0:2, :]
            yphi[x, 2 * k:2 * k + 2, :] = field[x, k, 30:32, :]
            head = field[x, k, :, 0:128]
            tail = field[x, k, :, 128:256]
            if k:
                head = pltpu.roll(head, 8 * k, 1)
                tail = pltpu.roll(tail, 8 * k, 1)
            left = jnp.where((lane >= 8 * k) & (lane < 8 * k + 2), head, left)
            low = (8 * k - 2) % 128
            right = jnp.where((lane >= low) & (lane < low + 2), tail, right)
        zplo[x] = left
        zphi[x] = right
        return carry

    def inner(x, carry):
        highs, lows = [], []
        for a in range(4):
            high, low = halves(field[x, :, 8 * a:8 * a + 8, :].reshape(128, 256))
            highs.append(high)
            lows.append(low)
        high = jnp.concatenate(highs, axis=1)
        both = jnp.concatenate([high, jnp.concatenate(lows, axis=1)], axis=0)
        total[...] += lax.dot_general(both, both, NT, preferred_element_type=F32)
        return carry

    total[...] = jnp.zeros_like(total)
    for part in range(parts):
        span = pl.ds(part * each, each)
        lax.fori_loop(part * each, (part + 1) * each, plane, 0)
        copies += [
            remote(yplo.at[span], yhi.at[span], ys.at[2 * part], yr.at[2 * part], "gy", 0),
            remote(yphi.at[span], ylo.at[span], ys.at[2 * part + 1], yr.at[2 * part + 1], "gy", 1),
            remote(zplo.at[span], zhi.at[span], zs.at[2 * part], zr.at[2 * part], "gz", 0),
            remote(zphi.at[span], zlo.at[span], zs.at[2 * part + 1], zr.at[2 * part + 1], "gz", 1),
        ]
    lax.fori_loop(0, planes, inner, 0)
    small = fold(total[...], 2)
    mine = (small[0:16, 0:16] + small[16:32, 16:32]) + (small[0:16, 16:32] + small[16:32, 0:16])
    gram[...] = unpack_square(sum_over_mesh(sizes, pack_square(mine), slots, gs, gr))
    for copy in copies:
        copy.wait()


def factor(gram):
    row = lax.broadcasted_iota(jnp.int32, (16, 32), 0)
    col = lax.broadcasted_iota(jnp.int32, (16, 32), 1)
    mat = jnp.concatenate([gram, (row == col).astype(F32)[:, 0:16]], axis=1)
    for j in range(16):
        scale = lax.rsqrt(mat[j:j + 1, j:j + 1])
        top = mat[j:j + 1, :] * scale
        side = jnp.where(row[:, 0:1] > j, mat[:, j:j + 1] * scale, 0.0)
        mat = jnp.where(row == j, top, mat - side * top)
    upper = jnp.where(col[:, 0:16] >= row[:, 0:16], mat[:, 0:16], 0.0)
    return upper, mat[:, 16:32]


def jacobi_round(first, second):
    lane = lax.broadcasted_iota(jnp.int32, (8, 32), 1)
    sub = lax.broadcasted_iota(jnp.int32, (8, 32), 0)
    inside = lane < 16
    masked_first = jnp.where(inside, first, 0.0)
    masked_second = jnp.where(inside, second, 0.0)
    app = jnp.sum(masked_first * first, axis=1, keepdims=True)
    aqq = jnp.sum(masked_second * second, axis=1, keepdims=True)
    apq = jnp.sum(masked_first * second, axis=1, keepdims=True)
    tau = aqq - app
    square = tau * tau + 4.0 * apq * apq
    live = square > 0
    inverse = lax.rsqrt(jnp.where(live, square, 1.0))
    cos2 = 0.5 + 0.5 * jnp.abs(tau) * inverse
    root = lax.rsqrt(cos2)
    cosine = jnp.where(live, cos2 * root, 1.0)
    signed = jnp.where(tau >= 0, apq, -apq)
    sine = jnp.where(live, signed * inverse * root, 0.0)
    new_first = cosine * first - sine * second
    new_second = sine * first + cosine * second
    down = pltpu.roll(new_first, 1, 0)
    up = pltpu.roll(new_second, 7, 0)
    entering = pltpu.roll(new_second, 1, 0)
    top = jnp.where(sub == 0, new_first, jnp.where(sub == 1, entering, down))
    bottom = jnp.where(sub == 7, new_first, up)
    return top, bottom


def jacobi_start(upper):
    eye = (
        lax.broadcasted_iota(jnp.int32, (16, 16), 0) == lax.broadcasted_iota(jnp.int32, (16, 16), 1)
    ).astype(F32)
    both = jnp.concatenate([upper, eye], axis=1)
    return both[0:8], jnp.concatenate([both[i:i + 1] for i in range(15, 7, -1)], axis=0)


def spectrum(first, second, norm, ncell, upper, lower_inverse):
    both = jnp.concatenate([first, second], axis=0)
    scaled = both[:, 0:16]
    vecs = both[:, 16:32]
    lam = jnp.sum(scaled * scaled, axis=1, keepdims=True)
    row = lax.broadcasted_iota(jnp.int32, (16, 16), 0)
    col = lax.broadcasted_iota(jnp.int32, (16, 16), 1)
    along = jnp.sum(jnp.where(row == col, lam, 0.0), axis=0, keepdims=True)
    above = (along > lam).astype(F32)
    ties = ((along == lam) & (col < row)).astype(F32)
    greater = jnp.sum(above, axis=1, keepdims=True)
    keep = (greater < RANK - 0.5).astype(F32)
    place = greater + jnp.sum(ties, axis=1, keepdims=True)
    sigma = jnp.sqrt(lam * (norm / ncell))
    sigmas = jnp.sum(jnp.where(place == col.astype(F32), sigma, 0.0), axis=0, keepdims=True)
    proj = lax.dot_general(vecs * keep, vecs, TN, precision=HIGH, preferred_element_type=F32)
    weights = keep / (lam * norm)
    inverse = lax.dot_general(vecs * weights, vecs, TN, precision=HIGH, preferred_element_type=F32)
    before = jnp.dot(proj, lower_inverse, precision=HIGH, preferred_element_type=F32)
    after = lax.dot_general(upper, inverse, TN, precision=HIGH, preferred_element_type=F32)
    return before, after, sigmas


def shift_kernel(
    ncell, snap, diff, xlo, xhi, ylo, yhi, zlo, zhi, gram,
    out, small, sigmas,
    field, total, edges, state, factors, sems,
):
    x = pl.program_id(0)
    planes = pl.num_programs(0)
    static_planes = field.shape[0] - 4

    def load(p, half):
        lanes = pl.ds(half * 128, 128)
        return pltpu.make_async_copy(
            snap.at[:, p, :, lanes], field.at[p + 2, :, half, pl.ds(8, 32)], sems.at[p + 2, half]
        )

    def edge(side, p, half):
        lanes = pl.ds(half * 128, 128)
        source = (xlo, xhi)[side]
        slot = p if side == 0 else static_planes + 2 + p
        return pltpu.make_async_copy(
            source.at[:, p, :, lanes], field.at[slot, :, half, pl.ds(8, 32)], sems.at[slot, half]
        )

    @pl.when(x == 0)
    def _():
        total[...] = jnp.zeros_like(total)
        for half in range(2):
            for p in range(2):
                edge(0, p, half).start()
        for p in range(static_planes):
            for half in range(2):
                load(p, half).start()
        for half in range(2):
            for p in range(2):
                edge(1, p, half).start()
        for half in range(2):
            for p in range(2):
                edge(0, p, half).wait()
                load(p, half).wait()

    @pl.when(x < planes - 2)
    def _():
        for half in range(2):
            load(x + 2, half).wait()

    @pl.when(x >= planes - 2)
    def _():
        for half in range(2):
            edge(1, x - (planes - 2), half).wait()

    lane32 = lax.broadcasted_iota(jnp.int32, (32, 128), 1)
    edges[...] = jnp.where(lane32 % 8 < 4, zhi[0], zlo[0])
    for k in range(SNAPS):
        for half in range(2):
            lanes = pl.ds(half * 128, 128)
            field[x + 2, k, half, 6:8, :] = ylo[0, 2 * k:2 * k + 2, lanes]
            field[x + 2, k, half, 40:42, :] = yhi[0, 2 * k:2 * k + 2, lanes]

    lane = lax.broadcasted_iota(jnp.int32, (8, 128), 1)

    def one(k):
        base = 128 - 8 * k
        for a in range(4):
            row = 8 + 8 * a

            def at(half, dx=0, dy=0):
                return field[x + 2 + dx, k, half, row + dy:row + dy + 8, :]

            centre = [at(0), at(1)]
            side = edges[8 * a:8 * a + 8, :]

            def moved(by):
                rolled = [pltpu.roll(c, by % 128, 1) for c in centre]
                outer = pltpu.roll(side, base + by, 1)
                if by > 0:
                    return [
                        jnp.where(lane < by, outer, rolled[0]),
                        jnp.where(lane < by, rolled[0], rolled[1]),
                    ]
                return [
                    jnp.where(lane >= 128 + by, rolled[1], rolled[0]),
                    jnp.where(lane >= 128 + by, outer, rolled[1]),
                ]

            zp1, zm1, zp2, zm2 = moved(-1), moved(1), moved(-2), moved(2)
            for half in range(2):
                u = centre[half]
                xp, xm, yp, ym = at(half, 1), at(half, -1), at(half, 0, 1), at(half, 0, -1)
                zp, zm = zp1[half], zm1[half]
                lap = ((xp + xm) + (yp + ym)) + ((zp + zm) - 6.0 * u)
                near = (xp - xm) + 0.75 * (yp - ym)
                far = (at(half, 2) - at(half, -2)) + 0.75 * (at(half, 0, 2) - at(half, 0, -2))
                steep = 8.0 * (zp - zm) - (zp2[half] - zm2[half])
                d = diff[0, 8 * a:8 * a + 8, half * 128:half * 128 + 128]
                new = (u + d * lap) - (0.3 / 12.0 + (0.02 / 12.0) * u) * steep
                new = new - ((1.6 / 12.0) * near - (0.2 / 12.0) * far)
                out[k, 0, 8 * a:8 * a + 8, half * 128:half * 128 + 128] = new

    def plain(i, carry):
        one(2 * i)
        one(2 * i + 1)
        return carry

    def turning(i, pair):
        one(2 * i)
        one(2 * i + 1)
        return jacobi_round(*pair)

    @pl.when(x == 0)
    def _():
        upper, lower_inverse = factor(gram[...])
        norm = jnp.sum(jnp.sum(upper * upper, axis=1, keepdims=True), axis=0, keepdims=True)
        first, second = jacobi_start(upper * lax.rsqrt(norm))
        state[0:8, 0:32] = first
        state[8:16, 0:32] = second
        factors[:, 0:16] = upper
        factors[:, 16:32] = lower_inverse

    @pl.when(x < planes - 1)
    def _():
        first, second = lax.fori_loop(0, 6, turning, (state[0:8, 0:32], state[8:16, 0:32]))
        state[0:8, 0:32] = first
        state[8:16, 0:32] = second
        lax.fori_loop(6, SNAPS // 2, plain, 0)

    @pl.when(x == planes - 1)
    def _():
        upper = factors[:, 0:16]
        lower_inverse = factors[:, 16:32]
        norm = jnp.sum(jnp.sum(upper * upper, axis=1, keepdims=True), axis=0, keepdims=True)
        small[0:16, 0:16], small[16:32, 0:16], sigmas[...] = spectrum(
            state[0:8, 0:32], state[8:16, 0:32], norm, ncell, upper, lower_inverse
        )
        lax.fori_loop(0, SNAPS // 2, plain, 0)

    xh, xl, yh, yl = [], [], [], []
    for a in range(4):
        for half in range(2):
            high, low = halves(
                field[x + 2, :, half, 8 + 8 * a:16 + 8 * a, :].reshape(128, 128)
            )
            xh.append(high)
            xl.append(low)
            high, low = halves(
                out[:, 0, 8 * a:8 * a + 8, half * 128:half * 128 + 128].reshape(128, 128)
            )
            yh.append(high)
            yl.append(low)
    cat = functools.partial(jnp.concatenate, axis=1)
    total[...] += lax.dot_general(
        jnp.concatenate([cat(yh), cat(yl)], axis=0),
        jnp.concatenate([cat(xh), cat(xl)], axis=0),
        NT, preferred_element_type=F32,
    )

    @pl.when(x == planes - 1)
    def _():
        sums = fold(total[...], 2)
        turned = (sums[0:16, 0:16] + sums[0:16, 16:32]) + (sums[16:32, 0:16] + sums[16:32, 16:32])
        small[32:40, 0:32] = pack_square(turned)


def finish_kernel(sizes, source, reduced, small, slots, load_sem, gs, gr):
    load = pltpu.make_async_copy(source, small, load_sem.at[0])
    load.start()
    enter(sizes)
    load.wait()
    turned = unpack_square(sum_over_mesh(sizes, small[32:40, 0:32], slots, gs, gr))
    inner = lax.dot_general(
        small[0:16, 0:16], turned, NT, precision=HIGH, preferred_element_type=F32
    )
    reduced[...] = jnp.dot(inner, small[16:32, 0:16], precision=HIGH, preferred_element_type=F32)


def shards(sizes, snapshots, diffusivity):
    planes = snapshots.shape[1]
    ncell = float(planes * 32 * 256 * sizes[0] * sizes[1] * sizes[2])
    hbm = pl.BlockSpec(memory_space=pltpu.HBM)
    vmem = pl.BlockSpec(memory_space=pltpu.VMEM)
    links = sum(count - 1 for count in sizes)
    dma = pltpu.SemaphoreType.DMA
    shape = functools.partial(jax.ShapeDtypeStruct, dtype=F32)
    *halos, gram = pl.pallas_call(
        functools.partial(exchange_kernel, sizes),
        name="exchange",
        out_shape=[
            shape((SNAPS, 2, 32, 256)), shape((SNAPS, 2, 32, 256)),
            shape((planes, 32, 256)), shape((planes, 32, 256)),
            shape((planes, 32, 128)), shape((planes, 32, 128)),
            shape((16, 16)),
        ],
        in_specs=[hbm],
        out_specs=[hbm] * 6 + [vmem],
        scratch_shapes=[
            pltpu.VMEM((planes, SNAPS, 32, 256), F32),
            pltpu.VMEM((planes, 32, 256), F32), pltpu.VMEM((planes, 32, 256), F32),
            pltpu.VMEM((planes, 32, 128), F32), pltpu.VMEM((planes, 32, 128), F32),
            pltpu.VMEM((256, 256), F32), pltpu.VMEM((24, 8, 128), F32),
            dma((planes,)), dma((2,)), dma((2,)), dma((8,)), dma((8,)), dma((8,)), dma((8,)),
            dma((links,)), dma((links,)),
        ],
        compiler_params=pltpu.CompilerParams(
            collective_id=0, has_side_effects=True, vmem_limit_bytes=62 << 20
        ),
    )(snapshots)
    row = lambda *block: pl.BlockSpec((1,) + block, lambda i: (i,) + (0,) * len(block))
    whole = lambda *block: pl.BlockSpec(block, lambda i: (0,) * len(block))
    shifted, small, sigmas = pl.pallas_call(
        functools.partial(shift_kernel, ncell),
        name="shift",
        grid=(planes,),
        out_shape=[
            shape(snapshots.shape), shape((40, 128)), shape((1, 16)),
        ],
        in_specs=[
            hbm, row(32, 256), hbm, hbm, row(32, 256), row(32, 256), row(32, 128), row(32, 128),
            whole(16, 16),
        ],
        out_specs=[
            pl.BlockSpec((SNAPS, 1, 32, 256), lambda i: (0, i, 0, 0)),
            whole(40, 128), whole(1, 16),
        ],
        scratch_shapes=[
            pltpu.VMEM((planes + 4, SNAPS, 2, 48, 128), F32),
            pltpu.VMEM((256, 256), F32), pltpu.VMEM((32, 128), F32),
            pltpu.VMEM((16, 128), F32), pltpu.VMEM((16, 128), F32),
            dma((planes + 4, 2)),
        ],
        compiler_params=pltpu.CompilerParams(vmem_limit_bytes=62 << 20),
    )(snapshots, diffusivity, *halos, gram)
    reduced = pl.pallas_call(
        functools.partial(finish_kernel, sizes),
        name="finish",
        out_shape=shape((16, 16)),
        in_specs=[hbm],
        out_specs=vmem,
        scratch_shapes=[
            pltpu.VMEM((40, 128), F32), pltpu.VMEM((24, 8, 128), F32),
            dma((1,)), dma((links,)), dma((links,)),
        ],
        compiler_params=pltpu.CompilerParams(collective_id=1, has_side_effects=True),
    )(small)
    return (shifted, reduced, sigmas.reshape(16))


def solution(mesh):
    sizes = tuple(mesh.shape[axis] for axis in AXES)
    return jax.shard_map(
        functools.partial(shards, sizes),
        mesh=mesh,
        in_specs=(P(None, "gx", "gy", "gz"), P("gx", "gy", "gz")),
        out_specs=(P(None, "gx", "gy", "gz"), P(), P()),
        check_vma=False,
    )
```

```python
import functools

import jax
import jax.numpy as jnp
import numpy as np
from jax import lax
from jax.experimental import pallas as pl
from jax.experimental.pallas import tpu as pltpu
from jax.sharding import PartitionSpec as P

SNAPS = 16
RANK = 12
SWEEPS = 6
HIGH = lax.Precision.HIGHEST
F32 = jnp.float32
BF16 = jnp.bfloat16
MESH = pl.DeviceIdType.MESH
AXES = ("gx", "gy", "gz")


def peers(sizes):
    found = []
    for axis, count in zip(AXES, sizes):
        for step in range(1, count):
            found.append((axis, lax.rem(lax.axis_index(axis) + step, count)))
    return found


def pack_square(square):
    return jnp.concatenate([square[0:8], square[8:16]], axis=1)


def unpack_square(packed):
    return jnp.concatenate([packed[:, 0:16], packed[:, 16:32]], axis=0)


def stage_copies(sizes, place, slots, send_sems, recv_sems):
    axis, count = AXES[place], sizes[place]
    me = lax.axis_index(axis)
    at = sum(size - 1 for size in sizes[:place])
    return [
        pltpu.make_async_remote_copy(
            src_ref=slots.at[8 * place + me],
            dst_ref=slots.at[8 * place + me],
            send_sem=send_sems.at[at + step - 1],
            recv_sem=recv_sems.at[at + step - 1],
            device_id={axis: lax.rem(me + step, count)},
            device_id_type=MESH,
        )
        for step in range(1, count)
    ]


def stage_start(sizes, place, value, slots, send_sems, recv_sems):
    slots[8 * place + lax.axis_index(AXES[place]), :, 0:32] = value
    for copy in stage_copies(sizes, place, slots, send_sems, recv_sems):
        copy.start()


def stage_finish(sizes, place, slots, send_sems, recv_sems):
    for copy in stage_copies(sizes, place, slots, send_sems, recv_sems):
        copy.wait()
    value = slots[8 * place, :, 0:32]
    for slot in range(1, sizes[place]):
        value = value + slots[8 * place + slot, :, 0:32]
    return value


def halves(block):
    high = block.astype(BF16)
    return high, (block - high.astype(F32)).astype(BF16)


def fold(total, groups):
    sub = lax.broadcasted_iota(jnp.int32, (8, 256), 0)
    lane = lax.broadcasted_iota(jnp.int32, (8, 256), 1)
    same = (sub == lane % 8).astype(F32)
    rows = jnp.sum(total.reshape(groups * 16, 8, 256) * same[None], axis=1)
    pick = (
        lax.broadcasted_iota(jnp.int32, (256, 32), 0) // 8
        == lax.broadcasted_iota(jnp.int32, (256, 32), 1)
    ).astype(F32)
    return jnp.dot(rows, pick, precision=HIGH, preferred_element_type=F32)


NT = (((1,), (1,)), ((), ()))
TN = (((0,), (0,)), ((), ()))


def factor(gram):
    row = lax.broadcasted_iota(jnp.int32, (16, 32), 0)
    col = lax.broadcasted_iota(jnp.int32, (16, 32), 1)
    mat = jnp.concatenate([gram, (row == col).astype(F32)[:, 0:16]], axis=1)
    for j in range(16):
        scale = lax.rsqrt(mat[j:j + 1, j:j + 1])
        top = mat[j:j + 1, :] * scale
        side = jnp.where(row[:, 0:1] > j, mat[:, j:j + 1] * scale, 0.0)
        mat = jnp.where(row == j, top, mat - side * top)
    upper = jnp.where(col[:, 0:16] >= row[:, 0:16], mat[:, 0:16], 0.0)
    return upper, mat[:, 16:32]


def jacobi_round(first, second):
    lane = lax.broadcasted_iota(jnp.int32, (8, 32), 1)
    sub = lax.broadcasted_iota(jnp.int32, (8, 32), 0)
    inside = lane < 16
    masked_first = jnp.where(inside, first, 0.0)
    masked_second = jnp.where(inside, second, 0.0)
    app = jnp.sum(masked_first * first, axis=1, keepdims=True)
    aqq = jnp.sum(masked_second * second, axis=1, keepdims=True)
    apq = jnp.sum(masked_first * second, axis=1, keepdims=True)
    tau = aqq - app
    square = tau * tau + 4.0 * apq * apq
    live = square > 0
    inverse = lax.rsqrt(jnp.where(live, square, 1.0))
    cos2 = 0.5 + 0.5 * jnp.abs(tau) * inverse
    root = lax.rsqrt(cos2)
    cosine = jnp.where(live, cos2 * root, 1.0)
    signed = jnp.where(tau >= 0, apq, -apq)
    sine = jnp.where(live, signed * inverse * root, 0.0)
    new_first = cosine * first - sine * second
    new_second = sine * first + cosine * second
    down = pltpu.roll(new_first, 1, 0)
    up = pltpu.roll(new_second, 7, 0)
    entering = pltpu.roll(new_second, 1, 0)
    top = jnp.where(sub == 0, new_first, jnp.where(sub == 1, entering, down))
    bottom = jnp.where(sub == 7, new_first, up)
    return top, bottom


def jacobi_start(upper):
    eye = (
        lax.broadcasted_iota(jnp.int32, (16, 16), 0) == lax.broadcasted_iota(jnp.int32, (16, 16), 1)
    ).astype(F32)
    both = jnp.concatenate([upper, eye], axis=1)
    return both[0:8], jnp.concatenate([both[i:i + 1] for i in range(15, 7, -1)], axis=0)


def spectrum(first, second, norm, ncell, upper, lower_inverse):
    both = jnp.concatenate([first, second], axis=0)
    scaled = both[:, 0:16]
    vecs = both[:, 16:32]
    lam = jnp.sum(scaled * scaled, axis=1, keepdims=True)
    row = lax.broadcasted_iota(jnp.int32, (16, 16), 0)
    col = lax.broadcasted_iota(jnp.int32, (16, 16), 1)
    along = jnp.sum(jnp.where(row == col, lam, 0.0), axis=0, keepdims=True)
    above = (along > lam).astype(F32)
    ties = ((along == lam) & (col < row)).astype(F32)
    greater = jnp.sum(above, axis=1, keepdims=True)
    keep = (greater < RANK - 0.5).astype(F32)
    place = greater + jnp.sum(ties, axis=1, keepdims=True)
    sigma = jnp.sqrt(lam * (norm / ncell))
    sigmas = jnp.sum(jnp.where(place == col.astype(F32), sigma, 0.0), axis=0, keepdims=True)
    proj = lax.dot_general(vecs * keep, vecs, TN, precision=HIGH, preferred_element_type=F32)
    weights = keep / (lam * norm)
    inverse = lax.dot_general(vecs * weights, vecs, TN, precision=HIGH, preferred_element_type=F32)
    before = jnp.dot(proj, lower_inverse, precision=HIGH, preferred_element_type=F32)
    after = lax.dot_general(upper, inverse, TN, precision=HIGH, preferred_element_type=F32)
    return before, after, sigmas


def slope_weights():
    base = np.zeros((260, 512), np.float32)
    for z in range(256):
        for step, lap, slope in ((-2, 0, 1), (-1, 1, -8), (0, -6, 0), (1, 1, 8), (2, 0, -1)):
            base[z + step + 2, z] += lap
            base[z + step + 2, 256 + z] += slope
    edge = base[[258, 259, 0, 1]]
    group = np.concatenate([edge, edge])
    return np.concatenate([base[2:258], base[2:258]] + [group] * 16)


JACOBI_AT = 8


def step_kernel(
    sizes, ncell, snap, diff, slope, out, reduced, sigmas,
    field, split, zbuf, weights, yplo, yphi, zplo, zphi, ylo, yhi, zlo, zhi, dbuf, obuf,
    gtotal, ctotal, state, factors, gslots, cslots,
    load_sem, aux_sem, out_sem, xs, xr, ys, yr, zs, zr, gs, gr, cs, cr,
):
    planes = dbuf.shape[0]
    parts = 4
    each = planes // parts

    def load(x, half):
        lanes = pl.ds(half * 128, 128)
        return pltpu.make_async_copy(
            snap.at[:, x, :, lanes], field.at[x + 2, :, half, pl.ds(8, 32)], load_sem.at[x, half]
        )

    for x in range(planes):
        for half in range(2):
            load(x, half).start()
    slope_copy = pltpu.make_async_copy(slope, weights, aux_sem.at[0])
    diff_copy = pltpu.make_async_copy(diff, dbuf, aux_sem.at[1])
    slope_copy.start()
    diff_copy.start()

    barrier = pltpu.get_barrier_semaphore()
    known = peers(sizes)
    for axis, target in known:
        pl.semaphore_signal(barrier, inc=1, device_id={axis: target}, device_id_type=MESH)
    near = {}
    for axis, count in zip(AXES, sizes):
        me = lax.axis_index(axis)
        near[axis] = (lax.rem(me + count - 1, count), lax.rem(me + 1, count))

    def remote(src, dst, send, recv, axis, side):
        return pltpu.make_async_remote_copy(
            src_ref=src, dst_ref=dst, send_sem=send, recv_sem=recv,
            device_id={axis: near[axis][side]}, device_id_type=MESH,
        )

    def x_copies():
        found = []
        for side in range(2):
            for p in range(2):
                for half in range(2):
                    source = p if side == 0 else planes - 2 + p
                    slot = planes + 2 + p if side == 0 else p
                    at = 4 * side + 2 * p + half
                    found.append(remote(
                        snap.at[:, source, :, pl.ds(half * 128, 128)],
                        field.at[slot, :, half, pl.ds(8, 32)],
                        xs.at[at], xr.at[at], "gx", side,
                    ))
        return found

    def yz_copies(part):
        span = pl.ds(part * each, each)
        a, b = 2 * part, 2 * part + 1
        return [
            remote(yplo.at[span], yhi.at[span], ys.at[a], yr.at[a], "gy", 0),
            remote(yphi.at[span], ylo.at[span], ys.at[b], yr.at[b], "gy", 1),
            remote(zplo.at[span], zhi.at[span], zs.at[a], zr.at[a], "gz", 0),
            remote(zphi.at[span], zlo.at[span], zs.at[b], zr.at[b], "gz", 1),
        ]

    lane = lax.broadcasted_iota(jnp.int32, (32, 128), 1)

    def pack(x, carry):
        for half in range(2):
            load(x, half).wait()
        left = jnp.zeros((32, 128), F32)
        right = jnp.zeros((32, 128), F32)
        for k in range(SNAPS):
            for half in range(2):
                lanes = pl.ds(half * 128, 128)
                yplo[x, 2 * k:2 * k + 2, lanes] = field[x + 2, k, half, 8:10, :]
                yphi[x, 2 * k:2 * k + 2, lanes] = field[x + 2, k, half, 38:40, :]
            head = field[x + 2, k, 0, 8:40, :]
            tail = pltpu.roll(field[x + 2, k, 1, 8:40, :], (8 * k + 4) % 128, 1)
            if k:
                head = pltpu.roll(head, 8 * k, 1)
            left = jnp.where((lane >= 8 * k) & (lane < 8 * k + 2), head, left)
            right = jnp.where((lane >= 8 * k + 2) & (lane < 8 * k + 4), tail, right)
        zplo[x] = left
        zphi[x] = right
        return carry

    def inner(x, carry):
        for a in range(4):
            for half in range(2):
                high, low = halves(
                    field[x + 2, :, half, 8 + 8 * a:16 + 8 * a, :].reshape(128, 128)
                )
                split[x, a, 0:128, half * 128:half * 128 + 128] = high
                split[x, a, 128:256, half * 128:half * 128 + 128] = low
        both = jnp.concatenate([split[x, a] for a in range(4)], axis=1)
        gtotal[...] += lax.dot_general(both, both, NT, preferred_element_type=F32)
        return carry

    gtotal[...] = jnp.zeros_like(gtotal)
    ctotal[...] = jnp.zeros_like(ctotal)
    for part in range(parts):
        lax.fori_loop(part * each, (part + 1) * each, pack, 0)
        if part == 0:
            pl.semaphore_wait(barrier, len(known))
            for copy in x_copies():
                copy.start()
        for copy in yz_copies(part):
            copy.start()
    lax.fori_loop(0, planes, inner, 0)
    sums = fold(gtotal[...], 2)
    mine = (sums[0:16, 0:16] + sums[16:32, 16:32]) + (sums[0:16, 16:32] + sums[16:32, 0:16])
    gram_args = (gslots, gs, gr)
    cross_args = (cslots, cs, cr)
    stage_start(sizes, 0, pack_square(mine), *gram_args)
    slope_copy.wait()
    diff_copy.wait()

    def write(x, slot):
        return pltpu.make_async_copy(obuf.at[slot], out.at[:, x], out_sem.at[slot])

    group = lax.broadcasted_iota(jnp.int32, (SNAPS, 8, 128), 0)
    own = lax.broadcasted_iota(jnp.int32, (SNAPS, 8, 128), 2) // 8 == group

    def rotate(rounds):
        first, second = lax.fori_loop(
            0, rounds, lambda i, pair: jacobi_round(*pair), (state[0:8, 0:32], state[8:16, 0:32])
        )
        state[0:8, 0:32] = first
        state[8:16, 0:32] = second

    def plane(i, carry):
        x = lax.rem(i + 2, planes)
        slot = lax.rem(i, 2)

        @pl.when(i == 0)
        def _():
            for copy in yz_copies(0):
                copy.wait()

        for part in range(1, parts):
            @pl.when(i == part * each - 2)
            def _(part=part):
                for copy in yz_copies(part):
                    copy.wait()

        @pl.when(i == planes - 4)
        def _():
            for copy in x_copies():
                copy.wait()

        @pl.when(i == JACOBI_AT - 6)
        def _():
            stage_start(sizes, 1, stage_finish(sizes, 0, *gram_args), *gram_args)

        @pl.when(i == JACOBI_AT - 3)
        def _():
            stage_start(sizes, 2, stage_finish(sizes, 1, *gram_args), *gram_args)

        @pl.when(i == JACOBI_AT)
        def _():
            upper, lower_inverse = factor(unpack_square(stage_finish(sizes, 2, *gram_args)))
            norm = jnp.sum(jnp.sum(upper * upper, axis=1, keepdims=True), axis=0, keepdims=True)
            first, second = jacobi_start(upper * lax.rsqrt(norm))
            state[0:8, 0:32] = first
            state[8:16, 0:32] = second
            factors[:, 0:16] = upper
            factors[:, 16:32] = lower_inverse

        @pl.when(i >= 2)
        def _():
            write(lax.rem(x + planes - 2, planes), slot).wait()

        outer = jnp.where(lane % 8 < 2, zhi[x], zlo[x])
        top = outer.astype(BF16).astype(F32)
        outer = jnp.where(lane % 8 < 4, top, pltpu.roll(outer - top, 4, 1))
        rows = []
        for a in range(4):
            edge = jnp.where(own, outer[8 * a:8 * a + 8, :][None], 0.0)
            rows.append(jnp.concatenate(
                [split[x, a, 0:128], split[x, a, 128:256], edge.reshape(128, 128).astype(BF16)],
                axis=1,
            ))
        zbuf[...] = jnp.dot(
            jnp.concatenate(rows, axis=0), weights[...], preferred_element_type=F32
        )
        for k in range(SNAPS):
            for half in range(2):
                lanes = pl.ds(half * 128, 128)
                field[x + 2, k, half, 6:8, :] = ylo[x, 2 * k:2 * k + 2, lanes]
                field[x + 2, k, half, 40:42, :] = yhi[x, 2 * k:2 * k + 2, lanes]

        def one(k):
            for a in range(4):
                row = 8 + 8 * a
                at_z = pl.ds(pl.multiple_of(128 * a + 8 * k, 8), 8)
                for half in range(2):
                    def at(dx, dy):
                        return field[x + 2 + dx, k, half, row + dy:row + dy + 8, :]

                    lanes = pl.ds(half * 128, 128)
                    u = at(0, 0)
                    xp, xm, yp, ym = at(1, 0), at(-1, 0), at(0, 1), at(0, -1)
                    lap = ((xp + xm) + (yp + ym)) + zbuf[at_z, lanes]
                    close = (xp - xm) + 0.75 * (yp - ym)
                    far = (at(2, 0) - at(-2, 0)) + 0.75 * (at(0, 2) - at(0, -2))
                    steep = zbuf[at_z, pl.ds(256 + half * 128, 128)]
                    new = (u + dbuf[x, 8 * a:8 * a + 8, lanes] * lap) - (
                        0.3 / 12.0 + (0.02 / 12.0) * u
                    ) * steep
                    new = new - ((1.6 / 12.0) * close - (0.2 / 12.0) * far)
                    obuf[slot, k, 8 * a:8 * a + 8, lanes] = new

        def plain(j, carry):
            one(2 * j)
            one(2 * j + 1)
            return carry

        def turning(j, pair):
            one(2 * j)
            one(2 * j + 1)
            return jacobi_round(*pair)

        @pl.when(i < JACOBI_AT)
        def _():
            lax.fori_loop(0, SNAPS // 2, plain, 0)

        @pl.when(i >= JACOBI_AT)
        def _():
            first, second = lax.fori_loop(
                0, SNAPS // 2, turning, (state[0:8, 0:32], state[8:16, 0:32])
            )
            state[0:8, 0:32] = first
            state[8:16, 0:32] = second

        write(x, slot).start()
        yh, yl = [], []
        for a in range(4):
            high, low = halves(obuf[slot, :, 8 * a:8 * a + 8, :].reshape(128, 256))
            yh.append(high)
            yl.append(low)
        cat = functools.partial(jnp.concatenate, axis=1)
        ctotal[...] += lax.dot_general(
            jnp.concatenate([cat(yh), cat(yl)], axis=0),
            cat([split[x, a] for a in range(4)]),
            NT, preferred_element_type=F32,
        )
        return carry

    lax.fori_loop(0, planes, plane, 0)
    left_over = SWEEPS * 15 - (planes - JACOBI_AT) * (SNAPS // 2)
    sums = fold(ctotal[...], 2)
    turned = (sums[0:16, 0:16] + sums[0:16, 16:32]) + (sums[16:32, 0:16] + sums[16:32, 16:32])
    stage_start(sizes, 0, pack_square(turned), *cross_args)
    rotate(left_over // 2)
    stage_start(sizes, 1, stage_finish(sizes, 0, *cross_args), *cross_args)
    rotate(left_over - left_over // 2)
    stage_start(sizes, 2, stage_finish(sizes, 1, *cross_args), *cross_args)
    upper = factors[:, 0:16]
    norm = jnp.sum(jnp.sum(upper * upper, axis=1, keepdims=True), axis=0, keepdims=True)
    before, after, sigmas[...] = spectrum(
        state[0:8, 0:32], state[8:16, 0:32], norm, ncell, upper, factors[:, 16:32]
    )
    for slot in range(2):
        write(slot, slot).wait()
    turned = unpack_square(stage_finish(sizes, 2, *cross_args))
    middle = lax.dot_general(before, turned, NT, precision=HIGH, preferred_element_type=F32)
    reduced[...] = jnp.dot(middle, after, precision=HIGH, preferred_element_type=F32)


def shards(sizes, snapshots, diffusivity):
    planes = snapshots.shape[1]
    ncell = float(planes * 32 * 256 * sizes[0] * sizes[1] * sizes[2])
    hbm = pl.BlockSpec(memory_space=pltpu.HBM)
    vmem = pl.BlockSpec(memory_space=pltpu.VMEM)
    links = sum(count - 1 for count in sizes)
    dma = pltpu.SemaphoreType.DMA
    shape = functools.partial(jax.ShapeDtypeStruct, dtype=F32)
    rows = [pltpu.VMEM((planes, 32, width), F32) for width in (256, 256, 128, 128)]
    shifted, reduced, sigmas = pl.pallas_call(
        functools.partial(step_kernel, sizes, ncell),
        name="step",
        out_shape=[shape(snapshots.shape), shape((16, 16)), shape((1, 16))],
        in_specs=[hbm] * 3,
        out_specs=[hbm, vmem, vmem],
        scratch_shapes=[
            pltpu.VMEM((planes + 4, SNAPS, 2, 48, 128), F32),
            pltpu.VMEM((planes, 4, 256, 256), BF16),
            pltpu.VMEM((512, 512), F32),
            pltpu.VMEM((640, 512), BF16),
            *rows,
            *rows,
            pltpu.VMEM((planes, 32, 256), F32),
            pltpu.VMEM((2, SNAPS, 32, 256), F32),
            pltpu.VMEM((256, 256), F32), pltpu.VMEM((256, 256), F32),
            pltpu.VMEM((16, 128), F32), pltpu.VMEM((16, 128), F32),
            pltpu.VMEM((24, 8, 128), F32), pltpu.VMEM((24, 8, 128), F32),
            dma((planes, 2)), dma((2,)), dma((2,)),
            *[dma((8,))] * 6,
            *[dma((links,))] * 4,
        ],
        compiler_params=pltpu.CompilerParams(
            collective_id=0, has_side_effects=True, vmem_limit_bytes=62 << 20
        ),
    )(snapshots, diffusivity, jnp.asarray(slope_weights(), BF16))
    return (shifted, reduced, sigmas.reshape(16))


def solution(mesh):
    sizes = tuple(mesh.shape[axis] for axis in AXES)
    return jax.shard_map(
        functools.partial(shards, sizes),
        mesh=mesh,
        in_specs=(P(None, "gx", "gy", "gz"), P("gx", "gy", "gz")),
        out_specs=(P(None, "gx", "gy", "gz"), P(), P()),
        check_vma=False,
    )
```

```python
import functools

import jax
import jax.numpy as jnp
import numpy as np
from jax import lax
from jax.experimental import pallas as pl
from jax.experimental.pallas import tpu as pltpu
from jax.sharding import PartitionSpec as P

SNAPS = 16
RANK = 12
SWEEPS = 6
HIGH = lax.Precision.HIGHEST
F32 = jnp.float32
BF16 = jnp.bfloat16
MESH = pl.DeviceIdType.MESH
AXES = ("gx", "gy", "gz")


def peers(sizes):
    found = []
    for axis, count in zip(AXES, sizes):
        for step in range(1, count):
            found.append((axis, lax.rem(lax.axis_index(axis) + step, count)))
    return found


def pack_square(square):
    return jnp.concatenate([square[0:8], square[8:16]], axis=1)


def unpack_square(packed):
    return jnp.concatenate([packed[:, 0:16], packed[:, 16:32]], axis=0)


def stage_copies(sizes, place, slots, send_sems, recv_sems):
    axis, count = AXES[place], sizes[place]
    me = lax.axis_index(axis)
    at = sum(size - 1 for size in sizes[:place])
    return [
        pltpu.make_async_remote_copy(
            src_ref=slots.at[8 * place + me],
            dst_ref=slots.at[8 * place + me],
            send_sem=send_sems.at[at + step - 1],
            recv_sem=recv_sems.at[at + step - 1],
            device_id={axis: lax.rem(me + step, count)},
            device_id_type=MESH,
        )
        for step in range(1, count)
    ]


def stage_start(sizes, place, value, slots, send_sems, recv_sems):
    slots[8 * place + lax.axis_index(AXES[place]), :, 0:32] = value
    for copy in stage_copies(sizes, place, slots, send_sems, recv_sems):
        copy.start()


def stage_finish(sizes, place, slots, send_sems, recv_sems):
    for copy in stage_copies(sizes, place, slots, send_sems, recv_sems):
        copy.wait()
    value = slots[8 * place, :, 0:32]
    for slot in range(1, sizes[place]):
        value = value + slots[8 * place + slot, :, 0:32]
    return value


def halves(block):
    high = block.astype(BF16)
    return high, (block - high.astype(F32)).astype(BF16)


def fold(total, groups):
    sub = lax.broadcasted_iota(jnp.int32, (8, 256), 0)
    lane = lax.broadcasted_iota(jnp.int32, (8, 256), 1)
    same = (sub == lane % 8).astype(F32)
    rows = jnp.sum(total.reshape(groups * 16, 8, 256) * same[None], axis=1)
    pick = (
        lax.broadcasted_iota(jnp.int32, (256, 32), 0) // 8
        == lax.broadcasted_iota(jnp.int32, (256, 32), 1)
    ).astype(F32)
    return jnp.dot(rows, pick, precision=HIGH, preferred_element_type=F32)


NT = (((1,), (1,)), ((), ()))
TN = (((0,), (0,)), ((), ()))


def factor(gram):
    row = lax.broadcasted_iota(jnp.int32, (16, 32), 0)
    col = lax.broadcasted_iota(jnp.int32, (16, 32), 1)
    mat = jnp.concatenate([gram, (row == col).astype(F32)[:, 0:16]], axis=1)
    for j in range(16):
        scale = lax.rsqrt(mat[j:j + 1, j:j + 1])
        top = mat[j:j + 1, :] * scale
        side = jnp.where(row[:, 0:1] > j, mat[:, j:j + 1] * scale, 0.0)
        mat = jnp.where(row == j, top, mat - side * top)
    upper = jnp.where(col[:, 0:16] >= row[:, 0:16], mat[:, 0:16], 0.0)
    return upper, mat[:, 16:32]


def jacobi_round(first, second):
    lane = lax.broadcasted_iota(jnp.int32, (8, 32), 1)
    sub = lax.broadcasted_iota(jnp.int32, (8, 32), 0)
    inside = lane < 16
    masked_first = jnp.where(inside, first, 0.0)
    masked_second = jnp.where(inside, second, 0.0)
    app = jnp.sum(masked_first * first, axis=1, keepdims=True)
    aqq = jnp.sum(masked_second * second, axis=1, keepdims=True)
    apq = jnp.sum(masked_first * second, axis=1, keepdims=True)
    tau = aqq - app
    square = tau * tau + 4.0 * apq * apq
    live = square > 0
    inverse = lax.rsqrt(jnp.where(live, square, 1.0))
    cos2 = 0.5 + 0.5 * jnp.abs(tau) * inverse
    root = lax.rsqrt(cos2)
    cosine = jnp.where(live, cos2 * root, 1.0)
    signed = jnp.where(tau >= 0, apq, -apq)
    sine = jnp.where(live, signed * inverse * root, 0.0)
    new_first = cosine * first - sine * second
    new_second = sine * first + cosine * second
    down = pltpu.roll(new_first, 1, 0)
    up = pltpu.roll(new_second, 7, 0)
    entering = pltpu.roll(new_second, 1, 0)
    top = jnp.where(sub == 0, new_first, jnp.where(sub == 1, entering, down))
    bottom = jnp.where(sub == 7, new_first, up)
    return top, bottom


def jacobi_start(upper):
    eye = (
        lax.broadcasted_iota(jnp.int32, (16, 16), 0) == lax.broadcasted_iota(jnp.int32, (16, 16), 1)
    ).astype(F32)
    both = jnp.concatenate([upper, eye], axis=1)
    return both[0:8], jnp.concatenate([both[i:i + 1] for i in range(15, 7, -1)], axis=0)


def spectrum(first, second, norm, ncell, upper, lower_inverse):
    both = jnp.concatenate([first, second], axis=0)
    scaled = both[:, 0:16]
    vecs = both[:, 16:32]
    lam = jnp.sum(scaled * scaled, axis=1, keepdims=True)
    row = lax.broadcasted_iota(jnp.int32, (16, 16), 0)
    col = lax.broadcasted_iota(jnp.int32, (16, 16), 1)
    along = jnp.sum(jnp.where(row == col, lam, 0.0), axis=0, keepdims=True)
    above = (along > lam).astype(F32)
    ties = ((along == lam) & (col < row)).astype(F32)
    greater = jnp.sum(above, axis=1, keepdims=True)
    keep = (greater < RANK - 0.5).astype(F32)
    place = greater + jnp.sum(ties, axis=1, keepdims=True)
    sigma = jnp.sqrt(lam * (norm / ncell))
    sigmas = jnp.sum(jnp.where(place == col.astype(F32), sigma, 0.0), axis=0, keepdims=True)
    proj = lax.dot_general(vecs * keep, vecs, TN, precision=HIGH, preferred_element_type=F32)
    weights = keep / (lam * norm)
    inverse = lax.dot_general(vecs * weights, vecs, TN, precision=HIGH, preferred_element_type=F32)
    before = jnp.dot(proj, lower_inverse, precision=HIGH, preferred_element_type=F32)
    after = lax.dot_general(upper, inverse, TN, precision=HIGH, preferred_element_type=F32)
    return before, after, sigmas


def slope_weights():
    base = np.zeros((132, 256), np.float32)
    for z in range(128):
        for step, lap, slope in ((-2, 0, 1), (-1, 1, -8), (0, -6, 0), (1, 1, 8), (2, 0, -1)):
            base[z + step + 2, z] += lap
            base[z + step + 2, 128 + z] += slope
    edge = base[[0, 1, 130, 131]]
    places = (np.arange(128) + 2) % 4
    return np.concatenate([base[2:130], base[2:130], edge[places]])


JACOBI_AT = 8


def step_kernel(
    sizes, ncell, snap, diff, slope, out, small,
    field, split, zbuf, ybuf, weights, yplo, yphi, zplo, zphi, ylo, yhi, zlo, zhi, mid, dbuf, obuf,
    gtotal, ctotal, state, factors, gslots, cslots,
    load_sem, aux_sem, out_sem, xs, xr, ys, yr, zs, zr, gs, gr, cs, cr,
):
    planes = dbuf.shape[0]
    parts = 4
    each = planes // parts

    def load(x, half):
        lanes = pl.ds(half * 128, 128)
        return pltpu.make_async_copy(
            snap.at[:, x, :, lanes], field.at[x + 2, :, half, pl.ds(8, 32)], load_sem.at[x, half]
        )

    for x in range(planes):
        for half in range(2):
            load(x, half).start()
    slope_copy = pltpu.make_async_copy(slope, weights, aux_sem.at[0])
    diff_copy = pltpu.make_async_copy(diff, dbuf, aux_sem.at[1])
    slope_copy.start()
    diff_copy.start()

    barrier = pltpu.get_barrier_semaphore()
    known = peers(sizes)
    for axis, target in known:
        pl.semaphore_signal(barrier, inc=1, device_id={axis: target}, device_id_type=MESH)
    near = {}
    for axis, count in zip(AXES, sizes):
        me = lax.axis_index(axis)
        near[axis] = (lax.rem(me + count - 1, count), lax.rem(me + 1, count))

    def remote(src, dst, send, recv, axis, side):
        return pltpu.make_async_remote_copy(
            src_ref=src, dst_ref=dst, send_sem=send, recv_sem=recv,
            device_id={axis: near[axis][side]}, device_id_type=MESH,
        )

    def x_copies():
        found = []
        for side in range(2):
            for p in range(2):
                for half in range(2):
                    source = p if side == 0 else planes - 2 + p
                    slot = planes + 2 + p if side == 0 else p
                    at = 4 * side + 2 * p + half
                    found.append(remote(
                        snap.at[:, source, :, pl.ds(half * 128, 128)],
                        field.at[slot, :, half, pl.ds(8, 32)],
                        xs.at[at], xr.at[at], "gx", side,
                    ))
        return found

    def yz_copies(part):
        span = pl.ds(part * each, each)
        a, b = 2 * part, 2 * part + 1
        return [
            remote(yplo.at[span], yhi.at[span], ys.at[a], yr.at[a], "gy", 0),
            remote(yphi.at[span], ylo.at[span], ys.at[b], yr.at[b], "gy", 1),
            remote(zplo.at[span], zhi.at[span], zs.at[a], zr.at[a], "gz", 0),
            remote(zphi.at[span], zlo.at[span], zs.at[b], zr.at[b], "gz", 1),
        ]

    lane = lax.broadcasted_iota(jnp.int32, (32, 128), 1)

    def pack(x, carry):
        for half in range(2):
            load(x, half).wait()
        left = jnp.zeros((32, 128), F32)
        right = jnp.zeros((32, 128), F32)
        centre = jnp.zeros((32, 128), F32)
        for k in range(SNAPS):
            for half in range(2):
                lanes = pl.ds(half * 128, 128)
                yplo[x, 2 * k:2 * k + 2, lanes] = field[x + 2, k, half, 8:10, :]
                yphi[x, 2 * k:2 * k + 2, lanes] = field[x + 2, k, half, 38:40, :]
            head = field[x + 2, k, 0, 8:40, :]
            tail = pltpu.roll(field[x + 2, k, 1, 8:40, :], (8 * k + 4) % 128, 1)
            if k:
                head = pltpu.roll(head, 8 * k, 1)
            left = jnp.where((lane >= 8 * k) & (lane < 8 * k + 2), head, left)
            right = jnp.where((lane >= 8 * k + 2) & (lane < 8 * k + 4), tail, right)
            centre = jnp.where((lane >= 8 * k + 4) & (lane < 8 * k + 6), tail, centre)
            low = (8 * k - 2) % 128
            centre = jnp.where((lane >= low) & (lane < low + 2), head, centre)
        zplo[x] = left
        zphi[x] = right
        mid[x] = centre
        for a in range(4):
            for half in range(2):
                high, low = halves(
                    field[x + 2, :, half, 8 + 8 * a:16 + 8 * a, :].reshape(128, 128)
                )
                split[x, a, 0:128, half * 128:half * 128 + 128] = high
                split[x, a, 128:256, half * 128:half * 128 + 128] = low
        both = jnp.concatenate([split[x, a] for a in range(4)], axis=1)
        gtotal[...] += lax.dot_general(both, both, NT, preferred_element_type=F32)
        return carry

    gtotal[...] = jnp.zeros_like(gtotal)
    ctotal[...] = jnp.zeros_like(ctotal)
    ybuf[...] = jnp.zeros_like(ybuf)
    for part in range(parts):
        lax.fori_loop(part * each, (part + 1) * each, pack, 0)
        if part == 0:
            pl.semaphore_wait(barrier, len(known))
            for copy in x_copies():
                copy.start()
        for copy in yz_copies(part):
            copy.start()
    sums = fold(gtotal[...], 2)
    mine = (sums[0:16, 0:16] + sums[16:32, 16:32]) + (sums[0:16, 16:32] + sums[16:32, 0:16])
    gram_args = (gslots, gs, gr)
    cross_args = (cslots, cs, cr)
    stage_start(sizes, 0, pack_square(mine), *gram_args)
    slope_copy.wait()
    diff_copy.wait()

    def write(x, slot):
        return pltpu.make_async_copy(obuf.at[slot], out.at[:, x], out_sem.at[slot])

    group = lax.broadcasted_iota(jnp.int32, (SNAPS, 8, 128), 0)
    own = (lax.broadcasted_iota(jnp.int32, (SNAPS, 8, 128), 2) + 2) % 128 // 8 == group

    def rotate(rounds):
        first, second = lax.fori_loop(
            0, rounds, lambda i, pair: jacobi_round(*pair), (state[0:8, 0:32], state[8:16, 0:32])
        )
        state[0:8, 0:32] = first
        state[8:16, 0:32] = second

    def cross(x):
        cat = functools.partial(jnp.concatenate, axis=1)
        ctotal[...] += lax.dot_general(
            cat([ybuf[a] for a in range(4)]), cat([split[x, a] for a in range(4)]),
            NT, preferred_element_type=F32,
        )

    def plane(i, carry):
        x = lax.rem(i + 2, planes)
        slot = lax.rem(i, 2)

        @pl.when(i == 0)
        def _():
            for copy in yz_copies(0):
                copy.wait()

        for part in range(1, parts):
            @pl.when(i == part * each - 2)
            def _(part=part):
                for copy in yz_copies(part):
                    copy.wait()

        @pl.when(i == planes - 4)
        def _():
            for copy in x_copies():
                copy.wait()

        @pl.when(i == JACOBI_AT - 6)
        def _():
            stage_start(sizes, 1, stage_finish(sizes, 0, *gram_args), *gram_args)

        @pl.when(i == JACOBI_AT - 3)
        def _():
            stage_start(sizes, 2, stage_finish(sizes, 1, *gram_args), *gram_args)

        @pl.when(i == JACOBI_AT)
        def _():
            upper, lower_inverse = factor(unpack_square(stage_finish(sizes, 2, *gram_args)))
            norm = jnp.sum(jnp.sum(upper * upper, axis=1, keepdims=True), axis=0, keepdims=True)
            first, second = jacobi_start(upper * lax.rsqrt(norm))
            state[0:8, 0:32] = first
            state[8:16, 0:32] = second
            factors[:, 0:16] = upper
            factors[:, 16:32] = lower_inverse

        @pl.when(i >= 2)
        def _():
            write(lax.rem(x + planes - 2, planes), slot).wait()

        cross(lax.rem(i + 1, planes))
        place = lane % 8
        outer = jnp.where(place < 2, zhi[x], jnp.where(place < 4, zlo[x], mid[x]))
        top = outer.astype(BF16).astype(F32)
        rest = outer - top
        inside = (place >= 2) & (place < 6)
        outer = [
            jnp.where(inside, top, pltpu.roll(rest, 124, 1)),
            jnp.where(inside, pltpu.roll(rest, 4, 1), top),
        ]
        rows = []
        for half in range(2):
            lanes = pl.ds(half * 128, 128)
            for a in range(4):
                edge = jnp.where(own, outer[half][8 * a:8 * a + 8, :][None], 0.0)
                rows.append(jnp.concatenate(
                    [
                        split[x, a, 0:128, lanes], split[x, a, 128:256, lanes],
                        edge.reshape(128, 128).astype(BF16),
                    ],
                    axis=1,
                ))
        zbuf[...] = jnp.dot(
            jnp.concatenate(rows, axis=0), weights[...], preferred_element_type=F32
        )
        for k in range(SNAPS):
            for half in range(2):
                lanes = pl.ds(half * 128, 128)
                field[x + 2, k, half, 6:8, :] = ylo[x, 2 * k:2 * k + 2, lanes]
                field[x + 2, k, half, 40:42, :] = yhi[x, 2 * k:2 * k + 2, lanes]

        def one(k, a, half):
            row = 8 + 8 * a
            at_z = pl.ds(pl.multiple_of(512 * half + 128 * a + 8 * k, 8), 8)

            def at(dx, dy):
                return field[x + 2 + dx, k, half, row + dy:row + dy + 8, :]

            lanes = pl.ds(half * 128, 128)
            u = at(0, 0)
            xp, xm, yp, ym = at(1, 0), at(-1, 0), at(0, 1), at(0, -1)
            lap = ((xp + xm) + (yp + ym)) + zbuf[at_z, 0:128]
            close = (xp - xm) + 0.75 * (yp - ym)
            far = (at(2, 0) - at(-2, 0)) + 0.75 * (at(0, 2) - at(0, -2))
            new = (u + dbuf[x, 8 * a:8 * a + 8, lanes] * lap) - (
                0.3 / 12.0 + (0.02 / 12.0) * u
            ) * zbuf[at_z, 128:256]
            new = new - ((1.6 / 12.0) * close - (0.2 / 12.0) * far)
            obuf[slot, k, 8 * a:8 * a + 8, lanes] = new
            return new

        def fields(j):
            k = 2 * j
            for a in range(4):
                for half in range(2):
                    lanes = pl.ds(half * 128, 128)
                    high, low = halves(
                        jnp.concatenate([one(k, a, half), one(k + 1, a, half)], axis=0)
                    )
                    ybuf[a, pl.ds(pl.multiple_of(8 * k, 16), 16), lanes] = high
                    ybuf[a, pl.ds(pl.multiple_of(128 + 8 * k, 16), 16), lanes] = low

        def plain(j, carry):
            fields(j)
            return carry

        def turning(j, pair):
            fields(j)
            return jacobi_round(*pair)

        @pl.when(i < JACOBI_AT)
        def _():
            lax.fori_loop(0, SNAPS // 2, plain, 0)

        @pl.when(i >= JACOBI_AT)
        def _():
            first, second = lax.fori_loop(
                0, SNAPS // 2, turning, (state[0:8, 0:32], state[8:16, 0:32])
            )
            state[0:8, 0:32] = first
            state[8:16, 0:32] = second

        write(x, slot).start()
        return carry

    lax.fori_loop(0, planes, plane, 0)
    cross(1)
    left_over = SWEEPS * 15 - (planes - JACOBI_AT) * (SNAPS // 2)
    sums = fold(ctotal[...], 2)
    turned = (sums[0:16, 0:16] + sums[0:16, 16:32]) + (sums[16:32, 0:16] + sums[16:32, 16:32])
    stage_start(sizes, 0, pack_square(turned), *cross_args)
    rotate(left_over // 2)
    stage_start(sizes, 1, stage_finish(sizes, 0, *cross_args), *cross_args)
    rotate(left_over - left_over // 2)
    stage_start(sizes, 2, stage_finish(sizes, 1, *cross_args), *cross_args)
    upper = factors[:, 0:16]
    norm = jnp.sum(jnp.sum(upper * upper, axis=1, keepdims=True), axis=0, keepdims=True)
    before, after, small[16:17, 0:16] = spectrum(
        state[0:8, 0:32], state[8:16, 0:32], norm, ncell, upper, factors[:, 16:32]
    )
    for slot in range(2):
        write(slot, slot).wait()
    turned = unpack_square(stage_finish(sizes, 2, *cross_args))
    middle = lax.dot_general(before, turned, NT, precision=HIGH, preferred_element_type=F32)
    small[0:16, 0:16] = jnp.dot(middle, after, precision=HIGH, preferred_element_type=F32)


def emit_kernel(held, small, out, reduced, sigmas, sem):
    copies = [
        pltpu.make_async_copy(held.at[k], out.at[k], sem.at[k]) for k in range(SNAPS)
    ]
    for copy in copies:
        copy.start()
    reduced[...] = small[0:16, 0:16]
    sigmas[...] = small[16:17, 0:16]
    for copy in copies:
        copy.wait()


def shards(sizes, snapshots, diffusivity):
    planes = snapshots.shape[1]
    ncell = float(planes * 32 * 256 * sizes[0] * sizes[1] * sizes[2])
    hbm = pl.BlockSpec(memory_space=pltpu.HBM)
    vmem = pl.BlockSpec(memory_space=pltpu.VMEM)
    links = sum(count - 1 for count in sizes)
    dma = pltpu.SemaphoreType.DMA
    shape = functools.partial(jax.ShapeDtypeStruct, dtype=F32)
    rows = [pltpu.VMEM((planes, 32, width), F32) for width in (256, 256, 128, 128)]
    held, small = pl.pallas_call(
        functools.partial(step_kernel, sizes, ncell),
        name="step",
        out_shape=[shape(snapshots.shape), shape((24, 128))],
        in_specs=[hbm] * 3,
        out_specs=[pl.BlockSpec(memory_space=pl.ANY), vmem],
        scratch_shapes=[
            pltpu.VMEM((planes + 4, SNAPS, 2, 48, 128), F32),
            pltpu.VMEM((planes, 4, 256, 256), BF16),
            pltpu.VMEM((1024, 256), F32),
            pltpu.VMEM((4, 256, 256), BF16),
            pltpu.VMEM((384, 256), BF16),
            *rows,
            *rows,
            pltpu.VMEM((planes, 32, 128), F32),
            pltpu.VMEM((planes, 32, 256), F32),
            pltpu.VMEM((2, SNAPS, 32, 256), F32),
            pltpu.VMEM((256, 256), F32), pltpu.VMEM((256, 256), F32),
            pltpu.VMEM((16, 128), F32), pltpu.VMEM((16, 128), F32),
            pltpu.VMEM((24, 8, 128), F32), pltpu.VMEM((24, 8, 128), F32),
            dma((planes, 2)), dma((2,)), dma((2,)),
            *[dma((8,))] * 6,
            *[dma((links,))] * 4,
        ],
        compiler_params=pltpu.CompilerParams(
            collective_id=0, has_side_effects=True, vmem_limit_bytes=42 << 20
        ),
    )(
        snapshots,
        pltpu.with_memory_space_constraint(diffusivity, pltpu.HBM),
        pltpu.with_memory_space_constraint(jnp.asarray(slope_weights(), BF16), pltpu.HBM),
    )
    shifted, reduced, sigmas = pl.pallas_call(
        emit_kernel,
        name="emit",
        out_shape=[shape(snapshots.shape), shape((16, 16)), shape((1, 16))],
        in_specs=[pl.BlockSpec(memory_space=pl.ANY), vmem],
        out_specs=[hbm, vmem, vmem],
        scratch_shapes=[dma((SNAPS,))],
        compiler_params=pltpu.CompilerParams(vmem_limit_bytes=4 << 20),
    )(held, small)
    return (shifted, reduced, sigmas.reshape(16))


def solution(mesh):
    sizes = tuple(mesh.shape[axis] for axis in AXES)
    return jax.shard_map(
        functools.partial(shards, sizes),
        mesh=mesh,
        in_specs=(P(None, "gx", "gy", "gz"), P("gx", "gy", "gz")),
        out_specs=(P(None, "gx", "gy", "gz"), P(), P()),
        check_vma=False,
    )
```

```python
import functools

import jax
import jax.numpy as jnp
import numpy as np
from jax import lax
from jax.experimental import pallas as pl
from jax.experimental.pallas import tpu as pltpu
from jax.sharding import PartitionSpec as P

SNAPS = 16
RANK = 12
SWEEPS = 6
HIGH = lax.Precision.HIGHEST
F32 = jnp.float32
BF16 = jnp.bfloat16
MESH = pl.DeviceIdType.MESH
AXES = ("gx", "gy", "gz")


def peers(sizes):
    found = []
    for axis, count in zip(AXES, sizes):
        for step in range(1, count):
            found.append((axis, lax.rem(lax.axis_index(axis) + step, count)))
    return found


def pack_square(square):
    return jnp.concatenate([square[0:8], square[8:16]], axis=1)


def unpack_square(packed):
    return jnp.concatenate([packed[:, 0:16], packed[:, 16:32]], axis=0)


def stage_copies(sizes, place, slots, send_sems, recv_sems):
    axis, count = AXES[place], sizes[place]
    me = lax.axis_index(axis)
    at = sum(size - 1 for size in sizes[:place])
    return [
        pltpu.make_async_remote_copy(
            src_ref=slots.at[8 * place + me],
            dst_ref=slots.at[8 * place + me],
            send_sem=send_sems.at[at + step - 1],
            recv_sem=recv_sems.at[at + step - 1],
            device_id={axis: lax.rem(me + step, count)},
            device_id_type=MESH,
        )
        for step in range(1, count)
    ]


def stage_start(sizes, place, value, slots, send_sems, recv_sems):
    slots[8 * place + lax.axis_index(AXES[place]), :, 0:32] = value
    for copy in stage_copies(sizes, place, slots, send_sems, recv_sems):
        copy.start()


def stage_finish(sizes, place, slots, send_sems, recv_sems):
    for copy in stage_copies(sizes, place, slots, send_sems, recv_sems):
        copy.wait()
    value = slots[8 * place, :, 0:32]
    for slot in range(1, sizes[place]):
        value = value + slots[8 * place + slot, :, 0:32]
    return value


def halves(block):
    high = block.astype(BF16)
    return high, (block - high.astype(F32)).astype(BF16)


def fold(total, groups):
    sub = lax.broadcasted_iota(jnp.int32, (8, 256), 0)
    lane = lax.broadcasted_iota(jnp.int32, (8, 256), 1)
    same = (sub == lane % 8).astype(F32)
    rows = jnp.sum(total.reshape(groups * 16, 8, 256) * same[None], axis=1)
    pick = (
        lax.broadcasted_iota(jnp.int32, (256, 32), 0) // 8
        == lax.broadcasted_iota(jnp.int32, (256, 32), 1)
    ).astype(F32)
    return jnp.dot(rows, pick, precision=HIGH, preferred_element_type=F32)


NT = (((1,), (1,)), ((), ()))
TN = (((0,), (0,)), ((), ()))


def factor(gram):
    row = lax.broadcasted_iota(jnp.int32, (16, 32), 0)
    col = lax.broadcasted_iota(jnp.int32, (16, 32), 1)
    mat = jnp.concatenate([gram, (row == col).astype(F32)[:, 0:16]], axis=1)
    for j in range(16):
        scale = lax.rsqrt(mat[j:j + 1, j:j + 1])
        top = mat[j:j + 1, :] * scale
        side = jnp.where(row[:, 0:1] > j, mat[:, j:j + 1] * scale, 0.0)
        mat = jnp.where(row == j, top, mat - side * top)
    upper = jnp.where(col[:, 0:16] >= row[:, 0:16], mat[:, 0:16], 0.0)
    return upper, mat[:, 16:32]


def jacobi_round(first, second):
    lane = lax.broadcasted_iota(jnp.int32, (8, 32), 1)
    sub = lax.broadcasted_iota(jnp.int32, (8, 32), 0)
    inside = lane < 16
    masked_first = jnp.where(inside, first, 0.0)
    masked_second = jnp.where(inside, second, 0.0)
    app = jnp.sum(masked_first * first, axis=1, keepdims=True)
    aqq = jnp.sum(masked_second * second, axis=1, keepdims=True)
    apq = jnp.sum(masked_first * second, axis=1, keepdims=True)
    tau = aqq - app
    square = tau * tau + 4.0 * apq * apq
    live = square > 0
    inverse = lax.rsqrt(jnp.where(live, square, 1.0))
    cos2 = 0.5 + 0.5 * jnp.abs(tau) * inverse
    root = lax.rsqrt(cos2)
    cosine = jnp.where(live, cos2 * root, 1.0)
    signed = jnp.where(tau >= 0, apq, -apq)
    sine = jnp.where(live, signed * inverse * root, 0.0)
    new_first = cosine * first - sine * second
    new_second = sine * first + cosine * second
    down = pltpu.roll(new_first, 1, 0)
    up = pltpu.roll(new_second, 7, 0)
    entering = pltpu.roll(new_second, 1, 0)
    top = jnp.where(sub == 0, new_first, jnp.where(sub == 1, entering, down))
    bottom = jnp.where(sub == 7, new_first, up)
    return top, bottom


def jacobi_start(upper):
    eye = (
        lax.broadcasted_iota(jnp.int32, (16, 16), 0) == lax.broadcasted_iota(jnp.int32, (16, 16), 1)
    ).astype(F32)
    both = jnp.concatenate([upper, eye], axis=1)
    return both[0:8], jnp.concatenate([both[i:i + 1] for i in range(15, 7, -1)], axis=0)


def spectrum(first, second, norm, ncell, upper, lower_inverse):
    both = jnp.concatenate([first, second], axis=0)
    scaled = both[:, 0:16]
    vecs = both[:, 16:32]
    lam = jnp.sum(scaled * scaled, axis=1, keepdims=True)
    row = lax.broadcasted_iota(jnp.int32, (16, 16), 0)
    col = lax.broadcasted_iota(jnp.int32, (16, 16), 1)
    along = jnp.sum(jnp.where(row == col, lam, 0.0), axis=0, keepdims=True)
    above = (along > lam).astype(F32)
    ties = ((along == lam) & (col < row)).astype(F32)
    greater = jnp.sum(above, axis=1, keepdims=True)
    keep = (greater < RANK - 0.5).astype(F32)
    place = greater + jnp.sum(ties, axis=1, keepdims=True)
    sigma = jnp.sqrt(lam * (norm / ncell))
    sigmas = jnp.sum(jnp.where(place == col.astype(F32), sigma, 0.0), axis=0, keepdims=True)
    proj = lax.dot_general(vecs * keep, vecs, TN, precision=HIGH, preferred_element_type=F32)
    weights = keep / (lam * norm)
    inverse = lax.dot_general(vecs * weights, vecs, TN, precision=HIGH, preferred_element_type=F32)
    before = jnp.dot(proj, lower_inverse, precision=HIGH, preferred_element_type=F32)
    after = lax.dot_general(upper, inverse, TN, precision=HIGH, preferred_element_type=F32)
    return before, after, sigmas


def slope_weights():
    base = np.zeros((132, 256), np.float32)
    for z in range(128):
        for step, lap, slope in ((-2, 0, 1), (-1, 1, -8), (0, -6, 0), (1, 1, 8), (2, 0, -1)):
            base[z + step + 2, z] += lap
            base[z + step + 2, 128 + z] += slope
    edge = base[[0, 1, 130, 131]]
    places = (np.arange(128) + 2) % 4
    return np.concatenate([base[2:130], base[2:130], edge[places]])


JACOBI_AT = 11


def step_kernel(
    sizes, ncell, snap, diff, slope, out, small,
    field, split, zbuf, ybuf, weights, yplo, yphi, zplo, zphi, ylo, yhi, zlo, zhi, mid, dbuf, obuf,
    gtotal, ctotal, state, factors, gslots, cslots,
    load_sem, aux_sem, out_sem, xs, xr, ys, yr, zs, zr, gs, gr, cs, cr,
):
    planes = dbuf.shape[0]
    parts = 4
    each = planes // parts

    def load(x, half):
        lanes = pl.ds(half * 128, 128)
        return pltpu.make_async_copy(
            snap.at[:, x, :, lanes], field.at[x + 2, :, half, pl.ds(8, 32)], load_sem.at[x, half]
        )

    for x in range(planes):
        for half in range(2):
            load(x, half).start()
    slope_copy = pltpu.make_async_copy(slope, weights, aux_sem.at[0])
    diff_copy = pltpu.make_async_copy(diff, dbuf, aux_sem.at[1])
    slope_copy.start()
    diff_copy.start()

    barrier = pltpu.get_barrier_semaphore()
    known = peers(sizes)
    for axis, target in known:
        pl.semaphore_signal(barrier, inc=1, device_id={axis: target}, device_id_type=MESH)
    near = {}
    for axis, count in zip(AXES, sizes):
        me = lax.axis_index(axis)
        near[axis] = (lax.rem(me + count - 1, count), lax.rem(me + 1, count))

    def remote(src, dst, send, recv, axis, side):
        return pltpu.make_async_remote_copy(
            src_ref=src, dst_ref=dst, send_sem=send, recv_sem=recv,
            device_id={axis: near[axis][side]}, device_id_type=MESH,
        )

    def x_copies():
        found = []
        for side in range(2):
            for p in range(2):
                for half in range(2):
                    source = p if side == 0 else planes - 2 + p
                    slot = planes + 2 + p if side == 0 else p
                    at = 4 * side + 2 * p + half
                    found.append(remote(
                        snap.at[:, source, :, pl.ds(half * 128, 128)],
                        field.at[slot, :, half, pl.ds(8, 32)],
                        xs.at[at], xr.at[at], "gx", side,
                    ))
        return found

    def yz_copies(part):
        span = pl.ds(part * each, each)
        a, b = 2 * part, 2 * part + 1
        return [
            remote(yplo.at[span], yhi.at[span], ys.at[a], yr.at[a], "gy", 0),
            remote(yphi.at[span], ylo.at[span], ys.at[b], yr.at[b], "gy", 1),
            remote(zplo.at[span], zhi.at[span], zs.at[a], zr.at[a], "gz", 0),
            remote(zphi.at[span], zlo.at[span], zs.at[b], zr.at[b], "gz", 1),
        ]

    lane = lax.broadcasted_iota(jnp.int32, (32, 128), 1)

    def pack(x, carry):
        for half in range(2):
            load(x, half).wait()
        left = jnp.zeros((32, 128), F32)
        right = jnp.zeros((32, 128), F32)
        centre = jnp.zeros((32, 128), F32)
        for k in range(SNAPS):
            for half in range(2):
                lanes = pl.ds(half * 128, 128)
                yplo[x, 2 * k:2 * k + 2, lanes] = field[x + 2, k, half, 8:10, :]
                yphi[x, 2 * k:2 * k + 2, lanes] = field[x + 2, k, half, 38:40, :]
            head = field[x + 2, k, 0, 8:40, :]
            tail = pltpu.roll(field[x + 2, k, 1, 8:40, :], (8 * k + 4) % 128, 1)
            if k:
                head = pltpu.roll(head, 8 * k, 1)
            left = jnp.where((lane >= 8 * k) & (lane < 8 * k + 2), head, left)
            right = jnp.where((lane >= 8 * k + 2) & (lane < 8 * k + 4), tail, right)
            centre = jnp.where((lane >= 8 * k + 4) & (lane < 8 * k + 6), tail, centre)
            low = (8 * k - 2) % 128
            centre = jnp.where((lane >= low) & (lane < low + 2), head, centre)
        zplo[x] = left
        zphi[x] = right
        mid[x] = centre
        for a in range(4):
            for half in range(2):
                high, low = halves(
                    field[x + 2, :, half, 8 + 8 * a:16 + 8 * a, :].reshape(128, 128)
                )
                split[x, a, 0:128, half * 128:half * 128 + 128] = high
                split[x, a, 128:256, half * 128:half * 128 + 128] = low
        both = jnp.concatenate([split[x, a] for a in range(4)], axis=1)
        gtotal[...] += lax.dot_general(both, both, NT, preferred_element_type=F32)
        return carry

    gtotal[...] = jnp.zeros_like(gtotal)
    ctotal[...] = jnp.zeros_like(ctotal)
    ybuf[...] = jnp.zeros_like(ybuf)
    for part in range(parts):
        lax.fori_loop(part * each, (part + 1) * each, pack, 0)
        if part == 0:
            pl.semaphore_wait(barrier, len(known))
            for copy in x_copies():
                copy.start()
        for copy in yz_copies(part):
            copy.start()
    sums = fold(gtotal[...], 2)
    mine = (sums[0:16, 0:16] + sums[16:32, 16:32]) + (sums[0:16, 16:32] + sums[16:32, 0:16])
    gram_args = (gslots, gs, gr)
    cross_args = (cslots, cs, cr)
    stage_start(sizes, 0, pack_square(mine), *gram_args)
    slope_copy.wait()
    diff_copy.wait()

    def write(x, slot):
        return pltpu.make_async_copy(obuf.at[slot], out.at[:, x], out_sem.at[slot])

    group = lax.broadcasted_iota(jnp.int32, (SNAPS, 8, 128), 0)
    own = (lax.broadcasted_iota(jnp.int32, (SNAPS, 8, 128), 2) + 2) % 128 // 8 == group

    def rotate(rounds):
        first, second = lax.fori_loop(
            0, rounds, lambda i, pair: jacobi_round(*pair), (state[0:8, 0:32], state[8:16, 0:32])
        )
        state[0:8, 0:32] = first
        state[8:16, 0:32] = second

    def cross(x):
        cat = functools.partial(jnp.concatenate, axis=1)
        ctotal[...] += lax.dot_general(
            cat([ybuf[a] for a in range(4)]), cat([split[x, a] for a in range(4)]),
            NT, preferred_element_type=F32,
        )

    def plane(i, carry):
        x = lax.rem(i + 2, planes)
        slot = lax.rem(i, 2)

        @pl.when(i == 0)
        def _():
            for copy in yz_copies(0):
                copy.wait()

        for part in range(1, parts):
            @pl.when(i == part * each - 2)
            def _(part=part):
                for copy in yz_copies(part):
                    copy.wait()

        @pl.when(i == planes - 4)
        def _():
            for copy in x_copies():
                copy.wait()

        @pl.when(i == JACOBI_AT - 6)
        def _():
            stage_start(sizes, 1, stage_finish(sizes, 0, *gram_args), *gram_args)

        @pl.when(i == JACOBI_AT - 3)
        def _():
            stage_start(sizes, 2, stage_finish(sizes, 1, *gram_args), *gram_args)

        @pl.when(i == JACOBI_AT)
        def _():
            upper, lower_inverse = factor(unpack_square(stage_finish(sizes, 2, *gram_args)))
            norm = jnp.sum(jnp.sum(upper * upper, axis=1, keepdims=True), axis=0, keepdims=True)
            first, second = jacobi_start(upper * lax.rsqrt(norm))
            state[0:8, 0:32] = first
            state[8:16, 0:32] = second
            factors[:, 0:16] = upper
            factors[:, 16:32] = lower_inverse

        @pl.when(i >= 2)
        def _():
            write(lax.rem(x + planes - 2, planes), slot).wait()

        cross(lax.rem(i + 1, planes))
        place = lane % 8
        outer = jnp.where(place < 2, zhi[x], jnp.where(place < 4, zlo[x], mid[x]))
        top = outer.astype(BF16).astype(F32)
        rest = outer - top
        inside = (place >= 2) & (place < 6)
        outer = [
            jnp.where(inside, top, pltpu.roll(rest, 124, 1)),
            jnp.where(inside, pltpu.roll(rest, 4, 1), top),
        ]
        rows = []
        for half in range(2):
            lanes = pl.ds(half * 128, 128)
            for a in range(4):
                edge = jnp.where(own, outer[half][8 * a:8 * a + 8, :][None], 0.0)
                rows.append(jnp.concatenate(
                    [
                        split[x, a, 0:128, lanes], split[x, a, 128:256, lanes],
                        edge.reshape(128, 128).astype(BF16),
                    ],
                    axis=1,
                ))
        zbuf[...] = jnp.dot(
            jnp.concatenate(rows, axis=0), weights[...], preferred_element_type=F32
        )
        for k in range(SNAPS):
            for half in range(2):
                lanes = pl.ds(half * 128, 128)
                field[x + 2, k, half, 6:8, :] = ylo[x, 2 * k:2 * k + 2, lanes]
                field[x + 2, k, half, 40:42, :] = yhi[x, 2 * k:2 * k + 2, lanes]

        def one(k, a, half):
            row = 8 + 8 * a
            at_z = pl.ds(pl.multiple_of(512 * half + 128 * a + 8 * k, 8), 8)

            def at(dx, dy):
                return field[x + 2 + dx, k, half, row + dy:row + dy + 8, :]

            lanes = pl.ds(half * 128, 128)
            u = at(0, 0)
            xp, xm, yp, ym = at(1, 0), at(-1, 0), at(0, 1), at(0, -1)
            lap = ((xp + xm) + (yp + ym)) + zbuf[at_z, 0:128]
            close = (xp - xm) + 0.75 * (yp - ym)
            far = (at(2, 0) - at(-2, 0)) + 0.75 * (at(0, 2) - at(0, -2))
            new = (u + dbuf[x, 8 * a:8 * a + 8, lanes] * lap) - (
                0.3 / 12.0 + (0.02 / 12.0) * u
            ) * zbuf[at_z, 128:256]
            new = new - ((1.6 / 12.0) * close - (0.2 / 12.0) * far)
            obuf[slot, k, 8 * a:8 * a + 8, lanes] = new
            return new

        def fields(j):
            k = 2 * j
            for a in range(4):
                for half in range(2):
                    lanes = pl.ds(half * 128, 128)
                    high, low = halves(
                        jnp.concatenate([one(k, a, half), one(k + 1, a, half)], axis=0)
                    )
                    ybuf[a, pl.ds(pl.multiple_of(8 * k, 16), 16), lanes] = high
                    ybuf[a, pl.ds(pl.multiple_of(128 + 8 * k, 16), 16), lanes] = low

        def plain(j, carry):
            fields(j)
            return carry

        def turning(j, pair):
            fields(j)
            return jacobi_round(*pair)

        @pl.when(i < JACOBI_AT)
        def _():
            lax.fori_loop(0, SNAPS // 2, plain, 0)

        @pl.when(i >= JACOBI_AT)
        def _():
            first, second = lax.fori_loop(
                0, SNAPS // 2, turning, (state[0:8, 0:32], state[8:16, 0:32])
            )
            state[0:8, 0:32] = first
            state[8:16, 0:32] = second

        write(x, slot).start()
        return carry

    lax.fori_loop(0, planes, plane, 0)
    cross(1)
    left_over = SWEEPS * 15 - (planes - JACOBI_AT) * (SNAPS // 2)
    sums = fold(ctotal[...], 2)
    turned = (sums[0:16, 0:16] + sums[0:16, 16:32]) + (sums[16:32, 0:16] + sums[16:32, 16:32])
    stage_start(sizes, 0, pack_square(turned), *cross_args)
    rotate(left_over // 2)
    stage_start(sizes, 1, stage_finish(sizes, 0, *cross_args), *cross_args)
    rotate(left_over - left_over // 2)
    stage_start(sizes, 2, stage_finish(sizes, 1, *cross_args), *cross_args)
    upper = factors[:, 0:16]
    norm = jnp.sum(jnp.sum(upper * upper, axis=1, keepdims=True), axis=0, keepdims=True)
    before, after, small[16:17, 0:16] = spectrum(
        state[0:8, 0:32], state[8:16, 0:32], norm, ncell, upper, factors[:, 16:32]
    )
    for slot in range(2):
        write(slot, slot).wait()
    turned = unpack_square(stage_finish(sizes, 2, *cross_args))
    middle = lax.dot_general(before, turned, NT, precision=HIGH, preferred_element_type=F32)
    small[0:16, 0:16] = jnp.dot(middle, after, precision=HIGH, preferred_element_type=F32)


def emit_kernel(held, small, out, reduced, sigmas, sem):
    copies = [
        pltpu.make_async_copy(held.at[k], out.at[k], sem.at[k]) for k in range(SNAPS)
    ]
    for copy in copies:
        copy.start()
    reduced[...] = small[0:16, 0:16]
    sigmas[...] = small[16:17, 0:16]
    for copy in copies:
        copy.wait()


def shards(sizes, snapshots, diffusivity):
    planes = snapshots.shape[1]
    ncell = float(planes * 32 * 256 * sizes[0] * sizes[1] * sizes[2])
    hbm = pl.BlockSpec(memory_space=pltpu.HBM)
    vmem = pl.BlockSpec(memory_space=pltpu.VMEM)
    links = sum(count - 1 for count in sizes)
    dma = pltpu.SemaphoreType.DMA
    shape = functools.partial(jax.ShapeDtypeStruct, dtype=F32)
    rows = [pltpu.VMEM((planes, 32, width), F32) for width in (256, 256, 128, 128)]
    held, small = pl.pallas_call(
        functools.partial(step_kernel, sizes, ncell),
        name="step",
        out_shape=[shape(snapshots.shape), shape((24, 128))],
        in_specs=[hbm] * 3,
        out_specs=[pl.BlockSpec(memory_space=pl.ANY), vmem],
        scratch_shapes=[
            pltpu.VMEM((planes + 4, SNAPS, 2, 48, 128), F32),
            pltpu.VMEM((planes, 4, 256, 256), BF16),
            pltpu.VMEM((1024, 256), F32),
            pltpu.VMEM((4, 256, 256), BF16),
            pltpu.VMEM((384, 256), BF16),
            *rows,
            *rows,
            pltpu.VMEM((planes, 32, 128), F32),
            pltpu.VMEM((planes, 32, 256), F32),
            pltpu.VMEM((2, SNAPS, 32, 256), F32),
            pltpu.VMEM((256, 256), F32), pltpu.VMEM((256, 256), F32),
            pltpu.VMEM((16, 128), F32), pltpu.VMEM((16, 128), F32),
            pltpu.VMEM((24, 8, 128), F32), pltpu.VMEM((24, 8, 128), F32),
            dma((planes, 2)), dma((2,)), dma((2,)),
            *[dma((8,))] * 6,
            *[dma((links,))] * 4,
        ],
        compiler_params=pltpu.CompilerParams(
            collective_id=0, has_side_effects=True, vmem_limit_bytes=42 << 20
        ),
    )(
        snapshots,
        pltpu.with_memory_space_constraint(diffusivity, pltpu.HBM),
        pltpu.with_memory_space_constraint(jnp.asarray(slope_weights(), BF16), pltpu.HBM),
    )
    shifted, reduced, sigmas = pl.pallas_call(
        emit_kernel,
        name="emit",
        out_shape=[shape(snapshots.shape), shape((16, 16)), shape((1, 16))],
        in_specs=[pl.BlockSpec(memory_space=pl.ANY), vmem],
        out_specs=[hbm, vmem, vmem],
        scratch_shapes=[dma((SNAPS,))],
        compiler_params=pltpu.CompilerParams(vmem_limit_bytes=4 << 20),
    )(held, small)
    return (shifted, reduced, sigmas.reshape(16))


def solution(mesh):
    sizes = tuple(mesh.shape[axis] for axis in AXES)
    return jax.shard_map(
        functools.partial(shards, sizes),
        mesh=mesh,
        in_specs=(P(None, "gx", "gy", "gz"), P("gx", "gy", "gz")),
        out_specs=(P(None, "gx", "gy", "gz"), P(), P()),
        check_vma=False,
    )
```

```python
import functools

import jax
import jax.numpy as jnp
import numpy as np
from jax import lax
from jax.experimental import pallas as pl
from jax.experimental.pallas import tpu as pltpu
from jax.sharding import PartitionSpec as P

SNAPS = 16
RANK = 12
SWEEPS = 6
HIGH = lax.Precision.HIGHEST
F32 = jnp.float32
BF16 = jnp.bfloat16
MESH = pl.DeviceIdType.MESH
AXES = ("gx", "gy", "gz")


def peers(sizes):
    found = []
    for axis, count in zip(AXES, sizes):
        for step in range(1, count):
            found.append((axis, lax.rem(lax.axis_index(axis) + step, count)))
    return found


def pack_square(square):
    return jnp.concatenate([square[0:8], square[8:16]], axis=1)


def unpack_square(packed):
    return jnp.concatenate([packed[:, 0:16], packed[:, 16:32]], axis=0)


def stage_copies(sizes, place, slots, send_sems, recv_sems):
    axis, count = AXES[place], sizes[place]
    me = lax.axis_index(axis)
    at = sum(size - 1 for size in sizes[:place])
    return [
        pltpu.make_async_remote_copy(
            src_ref=slots.at[8 * place + me],
            dst_ref=slots.at[8 * place + me],
            send_sem=send_sems.at[at + step - 1],
            recv_sem=recv_sems.at[at + step - 1],
            device_id={axis: lax.rem(me + step, count)},
            device_id_type=MESH,
        )
        for step in range(1, count)
    ]


def stage_start(sizes, place, value, slots, send_sems, recv_sems):
    slots[8 * place + lax.axis_index(AXES[place]), :, 0:32] = value
    for copy in stage_copies(sizes, place, slots, send_sems, recv_sems):
        copy.start()


def stage_finish(sizes, place, slots, send_sems, recv_sems):
    for copy in stage_copies(sizes, place, slots, send_sems, recv_sems):
        copy.wait()
    value = slots[8 * place, :, 0:32]
    for slot in range(1, sizes[place]):
        value = value + slots[8 * place + slot, :, 0:32]
    return value


def halves(block):
    high = block.astype(BF16)
    return high, (block - high.astype(F32)).astype(BF16)


def fold(total, groups):
    sub = lax.broadcasted_iota(jnp.int32, (8, 256), 0)
    lane = lax.broadcasted_iota(jnp.int32, (8, 256), 1)
    same = (sub == lane % 8).astype(F32)
    rows = jnp.sum(total.reshape(groups * 16, 8, 256) * same[None], axis=1)
    pick = (
        lax.broadcasted_iota(jnp.int32, (256, 32), 0) // 8
        == lax.broadcasted_iota(jnp.int32, (256, 32), 1)
    ).astype(F32)
    return jnp.dot(rows, pick, precision=HIGH, preferred_element_type=F32)


NT = (((1,), (1,)), ((), ()))
TN = (((0,), (0,)), ((), ()))


def factor(gram):
    row = lax.broadcasted_iota(jnp.int32, (16, 32), 0)
    col = lax.broadcasted_iota(jnp.int32, (16, 32), 1)
    mat = jnp.concatenate([gram, (row == col).astype(F32)[:, 0:16]], axis=1)
    for j in range(16):
        scale = lax.rsqrt(mat[j:j + 1, j:j + 1])
        top = mat[j:j + 1, :] * scale
        side = jnp.where(row[:, 0:1] > j, mat[:, j:j + 1] * scale, 0.0)
        mat = jnp.where(row == j, top, mat - side * top)
    upper = jnp.where(col[:, 0:16] >= row[:, 0:16], mat[:, 0:16], 0.0)
    return upper, mat[:, 16:32]


def jacobi_round(first, second):
    lane = lax.broadcasted_iota(jnp.int32, (8, 32), 1)
    sub = lax.broadcasted_iota(jnp.int32, (8, 32), 0)
    inside = lane < 16
    masked_first = jnp.where(inside, first, 0.0)
    masked_second = jnp.where(inside, second, 0.0)
    app = jnp.sum(masked_first * first, axis=1, keepdims=True)
    aqq = jnp.sum(masked_second * second, axis=1, keepdims=True)
    apq = jnp.sum(masked_first * second, axis=1, keepdims=True)
    tau = aqq - app
    square = tau * tau + 4.0 * apq * apq
    live = square > 0
    inverse = lax.rsqrt(jnp.where(live, square, 1.0))
    cos2 = 0.5 + 0.5 * jnp.abs(tau) * inverse
    root = lax.rsqrt(cos2)
    cosine = jnp.where(live, cos2 * root, 1.0)
    signed = jnp.where(tau >= 0, apq, -apq)
    sine = jnp.where(live, signed * inverse * root, 0.0)
    new_first = cosine * first - sine * second
    new_second = sine * first + cosine * second
    down = pltpu.roll(new_first, 1, 0)
    up = pltpu.roll(new_second, 7, 0)
    entering = pltpu.roll(new_second, 1, 0)
    top = jnp.where(sub == 0, new_first, jnp.where(sub == 1, entering, down))
    bottom = jnp.where(sub == 7, new_first, up)
    return top, bottom


def jacobi_start(upper):
    eye = (
        lax.broadcasted_iota(jnp.int32, (16, 16), 0) == lax.broadcasted_iota(jnp.int32, (16, 16), 1)
    ).astype(F32)
    both = jnp.concatenate([upper, eye], axis=1)
    return both[0:8], jnp.concatenate([both[i:i + 1] for i in range(15, 7, -1)], axis=0)


def spectrum(first, second, norm, ncell, upper, lower_inverse):
    both = jnp.concatenate([first, second], axis=0)
    scaled = both[:, 0:16]
    vecs = both[:, 16:32]
    lam = jnp.sum(scaled * scaled, axis=1, keepdims=True)
    row = lax.broadcasted_iota(jnp.int32, (16, 16), 0)
    col = lax.broadcasted_iota(jnp.int32, (16, 16), 1)
    along = jnp.sum(jnp.where(row == col, lam, 0.0), axis=0, keepdims=True)
    above = (along > lam).astype(F32)
    ties = ((along == lam) & (col < row)).astype(F32)
    greater = jnp.sum(above, axis=1, keepdims=True)
    keep = (greater < RANK - 0.5).astype(F32)
    place = greater + jnp.sum(ties, axis=1, keepdims=True)
    sigma = jnp.sqrt(lam * (norm / ncell))
    sigmas = jnp.sum(jnp.where(place == col.astype(F32), sigma, 0.0), axis=0, keepdims=True)
    proj = lax.dot_general(vecs * keep, vecs, TN, precision=HIGH, preferred_element_type=F32)
    weights = keep / (lam * norm)
    inverse = lax.dot_general(vecs * weights, vecs, TN, precision=HIGH, preferred_element_type=F32)
    before = jnp.dot(proj, lower_inverse, precision=HIGH, preferred_element_type=F32)
    after = lax.dot_general(upper, inverse, TN, precision=HIGH, preferred_element_type=F32)
    return before, after, sigmas


def slope_weights():
    base = np.zeros((132, 256), np.float32)
    for z in range(128):
        for step, lap, slope in ((-2, 0, 1), (-1, 1, -8), (0, -6, 0), (1, 1, 8), (2, 0, -1)):
            base[z + step + 2, z] += lap
            base[z + step + 2, 128 + z] += slope
    edge = base[[0, 1, 130, 131]]
    places = (np.arange(128) + 2) % 4
    return np.concatenate([base[2:130], base[2:130], edge[places]])


JACOBI_AT = 13


def step_kernel(
    sizes, ncell, snap, diff, slope, out, small,
    field, split, zbuf, ybuf, weights, yplo, yphi, zplo, zphi, ylo, yhi, zlo, zhi, mid, dbuf, obuf,
    gtotal, ctotal, state, factors, gslots, cslots,
    load_sem, aux_sem, out_sem, xs, xr, ys, yr, zs, zr, gs, gr, cs, cr,
):
    planes = dbuf.shape[0]
    parts = 4
    each = planes // parts

    def load(x, half):
        lanes = pl.ds(half * 128, 128)
        return pltpu.make_async_copy(
            snap.at[:, x, :, lanes], field.at[x + 2, :, half, pl.ds(8, 32)], load_sem.at[x, half]
        )

    for x in range(planes):
        for half in range(2):
            load(x, half).start()
    slope_copy = pltpu.make_async_copy(slope, weights, aux_sem.at[0])
    diff_copy = pltpu.make_async_copy(diff, dbuf, aux_sem.at[1])
    slope_copy.start()
    diff_copy.start()

    barrier = pltpu.get_barrier_semaphore()
    known = peers(sizes)
    for axis, target in known:
        pl.semaphore_signal(barrier, inc=1, device_id={axis: target}, device_id_type=MESH)
    near = {}
    for axis, count in zip(AXES, sizes):
        me = lax.axis_index(axis)
        near[axis] = (lax.rem(me + count - 1, count), lax.rem(me + 1, count))

    def remote(src, dst, send, recv, axis, side):
        return pltpu.make_async_remote_copy(
            src_ref=src, dst_ref=dst, send_sem=send, recv_sem=recv,
            device_id={axis: near[axis][side]}, device_id_type=MESH,
        )

    def x_copies():
        found = []
        for side in range(2):
            for p in range(2):
                for half in range(2):
                    source = p if side == 0 else planes - 2 + p
                    slot = planes + 2 + p if side == 0 else p
                    at = 4 * side + 2 * p + half
                    found.append(remote(
                        snap.at[:, source, :, pl.ds(half * 128, 128)],
                        field.at[slot, :, half, pl.ds(8, 32)],
                        xs.at[at], xr.at[at], "gx", side,
                    ))
        return found

    def yz_copies(part):
        span = pl.ds(part * each, each)
        a, b = 2 * part, 2 * part + 1
        return [
            remote(yplo.at[span], yhi.at[span], ys.at[a], yr.at[a], "gy", 0),
            remote(yphi.at[span], ylo.at[span], ys.at[b], yr.at[b], "gy", 1),
            remote(zplo.at[span], zhi.at[span], zs.at[a], zr.at[a], "gz", 0),
            remote(zphi.at[span], zlo.at[span], zs.at[b], zr.at[b], "gz", 1),
        ]

    lane = lax.broadcasted_iota(jnp.int32, (32, 128), 1)

    def pack(x, carry):
        for half in range(2):
            load(x, half).wait()
        left = jnp.zeros((32, 128), F32)
        right = jnp.zeros((32, 128), F32)
        centre = jnp.zeros((32, 128), F32)
        for k in range(SNAPS):
            for half in range(2):
                lanes = pl.ds(half * 128, 128)
                yplo[x, 2 * k:2 * k + 2, lanes] = field[x + 2, k, half, 8:10, :]
                yphi[x, 2 * k:2 * k + 2, lanes] = field[x + 2, k, half, 38:40, :]
            head = field[x + 2, k, 0, 8:40, :]
            tail = pltpu.roll(field[x + 2, k, 1, 8:40, :], (8 * k + 4) % 128, 1)
            if k:
                head = pltpu.roll(head, 8 * k, 1)
            left = jnp.where((lane >= 8 * k) & (lane < 8 * k + 2), head, left)
            right = jnp.where((lane >= 8 * k + 2) & (lane < 8 * k + 4), tail, right)
            centre = jnp.where((lane >= 8 * k + 4) & (lane < 8 * k + 6), tail, centre)
            low = (8 * k - 2) % 128
            centre = jnp.where((lane >= low) & (lane < low + 2), head, centre)
        zplo[x] = left
        zphi[x] = right
        mid[x] = centre
        for a in range(4):
            for half in range(2):
                high, low = halves(
                    field[x + 2, :, half, 8 + 8 * a:16 + 8 * a, :].reshape(128, 128)
                )
                split[x, a, 0:128, half * 128:half * 128 + 128] = high
                split[x, a, 128:256, half * 128:half * 128 + 128] = low
        both = jnp.concatenate([split[x, a] for a in range(4)], axis=1)
        gtotal[...] += lax.dot_general(both, both, NT, preferred_element_type=F32)
        return carry

    gtotal[...] = jnp.zeros_like(gtotal)
    ctotal[...] = jnp.zeros_like(ctotal)
    ybuf[...] = jnp.zeros_like(ybuf)
    for part in range(parts):
        lax.fori_loop(part * each, (part + 1) * each, pack, 0)
        if part == 0:
            pl.semaphore_wait(barrier, len(known))
            for copy in x_copies():
                copy.start()
        for copy in yz_copies(part):
            copy.start()
    sums = fold(gtotal[...], 2)
    mine = (sums[0:16, 0:16] + sums[16:32, 16:32]) + (sums[0:16, 16:32] + sums[16:32, 0:16])
    gram_args = (gslots, gs, gr)
    cross_args = (cslots, cs, cr)
    stage_start(sizes, 0, pack_square(mine), *gram_args)
    slope_copy.wait()
    diff_copy.wait()

    def write(x, slot):
        return pltpu.make_async_copy(obuf.at[slot], out.at[:, x], out_sem.at[slot])

    group = lax.broadcasted_iota(jnp.int32, (SNAPS, 8, 128), 0)
    own = (lax.broadcasted_iota(jnp.int32, (SNAPS, 8, 128), 2) + 2) % 128 // 8 == group

    def rotate(rounds):
        first, second = lax.fori_loop(
            0, rounds, lambda i, pair: jacobi_round(*pair), (state[0:8, 0:32], state[8:16, 0:32])
        )
        state[0:8, 0:32] = first
        state[8:16, 0:32] = second

    def cross(x):
        cat = functools.partial(jnp.concatenate, axis=1)
        ctotal[...] += lax.dot_general(
            cat([ybuf[a] for a in range(4)]), cat([split[x, a] for a in range(4)]),
            NT, preferred_element_type=F32,
        )

    def plane(i, carry):
        x = lax.rem(i + 2, planes)
        slot = lax.rem(i, 2)

        @pl.when(i == 0)
        def _():
            for copy in yz_copies(0):
                copy.wait()

        for part in range(1, parts):
            @pl.when(i == part * each - 2)
            def _(part=part):
                for copy in yz_copies(part):
                    copy.wait()

        @pl.when(i == planes - 4)
        def _():
            for copy in x_copies():
                copy.wait()

        @pl.when(i == JACOBI_AT - 5)
        def _():
            stage_start(sizes, 1, stage_finish(sizes, 0, *gram_args), *gram_args)

        @pl.when(i == JACOBI_AT - 2)
        def _():
            stage_start(sizes, 2, stage_finish(sizes, 1, *gram_args), *gram_args)

        @pl.when(i == JACOBI_AT)
        def _():
            upper, lower_inverse = factor(unpack_square(stage_finish(sizes, 2, *gram_args)))
            norm = jnp.sum(jnp.sum(upper * upper, axis=1, keepdims=True), axis=0, keepdims=True)
            first, second = jacobi_start(upper * lax.rsqrt(norm))
            state[0:8, 0:32] = first
            state[8:16, 0:32] = second
            factors[:, 0:16] = upper
            factors[:, 16:32] = lower_inverse

        @pl.when(i >= 2)
        def _():
            write(lax.rem(x + planes - 2, planes), slot).wait()

        cross(lax.rem(i + 1, planes))
        place = lane % 8
        outer = jnp.where(place < 2, zhi[x], jnp.where(place < 4, zlo[x], mid[x]))
        top = outer.astype(BF16).astype(F32)
        rest = outer - top
        inside = (place >= 2) & (place < 6)
        outer = [
            jnp.where(inside, top, pltpu.roll(rest, 124, 1)),
            jnp.where(inside, pltpu.roll(rest, 4, 1), top),
        ]
        rows = []
        for half in range(2):
            lanes = pl.ds(half * 128, 128)
            for a in range(4):
                edge = jnp.where(own, outer[half][8 * a:8 * a + 8, :][None], 0.0)
                rows.append(jnp.concatenate(
                    [
                        split[x, a, 0:128, lanes], split[x, a, 128:256, lanes],
                        edge.reshape(128, 128).astype(BF16),
                    ],
                    axis=1,
                ))
        zbuf[...] = jnp.dot(
            jnp.concatenate(rows, axis=0), weights[...], preferred_element_type=F32
        )
        for k in range(SNAPS):
            for half in range(2):
                lanes = pl.ds(half * 128, 128)
                field[x + 2, k, half, 6:8, :] = ylo[x, 2 * k:2 * k + 2, lanes]
                field[x + 2, k, half, 40:42, :] = yhi[x, 2 * k:2 * k + 2, lanes]

        def one(k, a, half):
            row = 8 + 8 * a
            at_z = pl.ds(pl.multiple_of(512 * half + 128 * a + 8 * k, 8), 8)

            def at(dx, dy):
                return field[x + 2 + dx, k, half, row + dy:row + dy + 8, :]

            lanes = pl.ds(half * 128, 128)
            u = at(0, 0)
            xp, xm, yp, ym = at(1, 0), at(-1, 0), at(0, 1), at(0, -1)
            lap = ((xp + xm) + (yp + ym)) + zbuf[at_z, 0:128]
            close = (xp - xm) + 0.75 * (yp - ym)
            far = (at(2, 0) - at(-2, 0)) + 0.75 * (at(0, 2) - at(0, -2))
            new = (u + dbuf[x, 8 * a:8 * a + 8, lanes] * lap) - (
                0.3 / 12.0 + (0.02 / 12.0) * u
            ) * zbuf[at_z, 128:256]
            new = new - ((1.6 / 12.0) * close - (0.2 / 12.0) * far)
            obuf[slot, k, 8 * a:8 * a + 8, lanes] = new
            return new

        def fields(j):
            k = 2 * j
            for a in range(4):
                for half in range(2):
                    lanes = pl.ds(half * 128, 128)
                    high, low = halves(
                        jnp.concatenate([one(k, a, half), one(k + 1, a, half)], axis=0)
                    )
                    ybuf[a, pl.ds(pl.multiple_of(8 * k, 16), 16), lanes] = high
                    ybuf[a, pl.ds(pl.multiple_of(128 + 8 * k, 16), 16), lanes] = low

        def plain(j, carry):
            fields(j)
            return carry

        def turning(j, pair):
            fields(j)
            return jacobi_round(*pair)

        @pl.when(i < JACOBI_AT)
        def _():
            lax.fori_loop(0, SNAPS // 2, plain, 0)

        @pl.when(i >= JACOBI_AT)
        def _():
            first, second = lax.fori_loop(
                0, SNAPS // 2, turning, (state[0:8, 0:32], state[8:16, 0:32])
            )
            state[0:8, 0:32] = first
            state[8:16, 0:32] = second

        write(x, slot).start()
        return carry

    lax.fori_loop(0, planes, plane, 0)
    cross(1)
    left_over = SWEEPS * 15 - (planes - JACOBI_AT) * (SNAPS // 2)
    sums = fold(ctotal[...], 2)
    turned = (sums[0:16, 0:16] + sums[0:16, 16:32]) + (sums[16:32, 0:16] + sums[16:32, 16:32])
    stage_start(sizes, 0, pack_square(turned), *cross_args)
    early, middle = left_over * 4 // 9, left_over // 3
    rotate(early)
    stage_start(sizes, 1, stage_finish(sizes, 0, *cross_args), *cross_args)
    rotate(middle)
    stage_start(sizes, 2, stage_finish(sizes, 1, *cross_args), *cross_args)
    rotate(left_over - early - middle)
    upper = factors[:, 0:16]
    norm = jnp.sum(jnp.sum(upper * upper, axis=1, keepdims=True), axis=0, keepdims=True)
    before, after, small[16:17, 0:16] = spectrum(
        state[0:8, 0:32], state[8:16, 0:32], norm, ncell, upper, factors[:, 16:32]
    )
    for slot in range(2):
        write(slot, slot).wait()
    turned = unpack_square(stage_finish(sizes, 2, *cross_args))
    middle = lax.dot_general(before, turned, NT, precision=HIGH, preferred_element_type=F32)
    small[0:16, 0:16] = jnp.dot(middle, after, precision=HIGH, preferred_element_type=F32)


def emit_kernel(held, small, out, reduced, sigmas, sem):
    copies = [
        pltpu.make_async_copy(held.at[k], out.at[k], sem.at[k]) for k in range(SNAPS)
    ]
    for copy in copies:
        copy.start()
    reduced[...] = small[0:16, 0:16]
    sigmas[...] = small[16:17, 0:16]
    for copy in copies:
        copy.wait()


def shards(sizes, snapshots, diffusivity):
    planes = snapshots.shape[1]
    ncell = float(planes * 32 * 256 * sizes[0] * sizes[1] * sizes[2])
    hbm = pl.BlockSpec(memory_space=pltpu.HBM)
    vmem = pl.BlockSpec(memory_space=pltpu.VMEM)
    links = sum(count - 1 for count in sizes)
    dma = pltpu.SemaphoreType.DMA
    shape = functools.partial(jax.ShapeDtypeStruct, dtype=F32)
    rows = [pltpu.VMEM((planes, 32, width), F32) for width in (256, 256, 128, 128)]
    held, small = pl.pallas_call(
        functools.partial(step_kernel, sizes, ncell),
        name="step",
        out_shape=[shape(snapshots.shape), shape((24, 128))],
        in_specs=[hbm] * 3,
        out_specs=[pl.BlockSpec(memory_space=pl.ANY), vmem],
        scratch_shapes=[
            pltpu.VMEM((planes + 4, SNAPS, 2, 48, 128), F32),
            pltpu.VMEM((planes, 4, 256, 256), BF16),
            pltpu.VMEM((1024, 256), F32),
            pltpu.VMEM((4, 256, 256), BF16),
            pltpu.VMEM((384, 256), BF16),
            *rows,
            *rows,
            pltpu.VMEM((planes, 32, 128), F32),
            pltpu.VMEM((planes, 32, 256), F32),
            pltpu.VMEM((2, SNAPS, 32, 256), F32),
            pltpu.VMEM((256, 256), F32), pltpu.VMEM((256, 256), F32),
            pltpu.VMEM((16, 128), F32), pltpu.VMEM((16, 128), F32),
            pltpu.VMEM((24, 8, 128), F32), pltpu.VMEM((24, 8, 128), F32),
            dma((planes, 2)), dma((2,)), dma((2,)),
            *[dma((8,))] * 6,
            *[dma((links,))] * 4,
        ],
        compiler_params=pltpu.CompilerParams(
            collective_id=0, has_side_effects=True, vmem_limit_bytes=42 << 20
        ),
    )(
        snapshots,
        pltpu.with_memory_space_constraint(diffusivity, pltpu.HBM),
        pltpu.with_memory_space_constraint(jnp.asarray(slope_weights(), BF16), pltpu.HBM),
    )
    shifted, reduced, sigmas = pl.pallas_call(
        emit_kernel,
        name="emit",
        out_shape=[shape(snapshots.shape), shape((16, 16)), shape((1, 16))],
        in_specs=[pl.BlockSpec(memory_space=pl.ANY), vmem],
        out_specs=[hbm, vmem, vmem],
        scratch_shapes=[dma((SNAPS,))],
        compiler_params=pltpu.CompilerParams(vmem_limit_bytes=4 << 20),
    )(held, small)
    return (shifted, reduced, sigmas.reshape(16))


def solution(mesh):
    sizes = tuple(mesh.shape[axis] for axis in AXES)
    return jax.shard_map(
        functools.partial(shards, sizes),
        mesh=mesh,
        in_specs=(P(None, "gx", "gy", "gz"), P("gx", "gy", "gz")),
        out_specs=(P(None, "gx", "gy", "gz"), P(), P()),
        check_vma=False,
    )
```

```python
import functools

import jax
import jax.numpy as jnp
import numpy as np
from jax import lax
from jax.experimental import pallas as pl
from jax.experimental.pallas import tpu as pltpu
from jax.sharding import PartitionSpec as P

SNAPS = 16
RANK = 12
SWEEPS = 6
HIGH = lax.Precision.HIGHEST
F32 = jnp.float32
BF16 = jnp.bfloat16
MESH = pl.DeviceIdType.MESH
AXES = ("gx", "gy", "gz")


def peers(sizes):
    found = []
    for axis, count in zip(AXES, sizes):
        for step in range(1, count):
            found.append((axis, lax.rem(lax.axis_index(axis) + step, count)))
    return found


def pack_square(square):
    return jnp.concatenate([square[0:8], square[8:16]], axis=1)


def unpack_square(packed):
    return jnp.concatenate([packed[:, 0:16], packed[:, 16:32]], axis=0)


def stage_copies(sizes, place, slots, send_sems, recv_sems):
    axis, count = AXES[place], sizes[place]
    me = lax.axis_index(axis)
    at = sum(size - 1 for size in sizes[:place])
    return [
        pltpu.make_async_remote_copy(
            src_ref=slots.at[8 * place + me],
            dst_ref=slots.at[8 * place + me],
            send_sem=send_sems.at[at + step - 1],
            recv_sem=recv_sems.at[at + step - 1],
            device_id={axis: lax.rem(me + step, count)},
            device_id_type=MESH,
        )
        for step in range(1, count)
    ]


def stage_start(sizes, place, value, slots, send_sems, recv_sems):
    slots[8 * place + lax.axis_index(AXES[place]), :, 0:32] = value
    for copy in stage_copies(sizes, place, slots, send_sems, recv_sems):
        copy.start()


def stage_finish(sizes, place, slots, send_sems, recv_sems):
    for copy in stage_copies(sizes, place, slots, send_sems, recv_sems):
        copy.wait()
    value = slots[8 * place, :, 0:32]
    for slot in range(1, sizes[place]):
        value = value + slots[8 * place + slot, :, 0:32]
    return value


def halves(block):
    high = block.astype(BF16)
    return high, (block - high.astype(F32)).astype(BF16)


def fold(total, groups):
    sub = lax.broadcasted_iota(jnp.int32, (8, 256), 0)
    lane = lax.broadcasted_iota(jnp.int32, (8, 256), 1)
    same = (sub == lane % 8).astype(F32)
    rows = jnp.sum(total.reshape(groups * 16, 8, 256) * same[None], axis=1)
    pick = (
        lax.broadcasted_iota(jnp.int32, (256, 32), 0) // 8
        == lax.broadcasted_iota(jnp.int32, (256, 32), 1)
    ).astype(F32)
    return jnp.dot(rows, pick, precision=HIGH, preferred_element_type=F32)


NT = (((1,), (1,)), ((), ()))
TN = (((0,), (0,)), ((), ()))


def factor(gram):
    row = lax.broadcasted_iota(jnp.int32, (16, 32), 0)
    col = lax.broadcasted_iota(jnp.int32, (16, 32), 1)
    mat = jnp.concatenate([gram, (row == col).astype(F32)[:, 0:16]], axis=1)
    for j in range(16):
        scale = lax.rsqrt(mat[j:j + 1, j:j + 1])
        top = mat[j:j + 1, :] * scale
        side = jnp.where(row[:, 0:1] > j, mat[:, j:j + 1] * scale, 0.0)
        mat = jnp.where(row == j, top, mat - side * top)
    upper = jnp.where(col[:, 0:16] >= row[:, 0:16], mat[:, 0:16], 0.0)
    return upper, mat[:, 16:32]


def jacobi_round(first, second):
    lane = lax.broadcasted_iota(jnp.int32, (8, 32), 1)
    sub = lax.broadcasted_iota(jnp.int32, (8, 32), 0)
    inside = lane < 16
    masked_first = jnp.where(inside, first, 0.0)
    masked_second = jnp.where(inside, second, 0.0)
    app = jnp.sum(masked_first * first, axis=1, keepdims=True)
    aqq = jnp.sum(masked_second * second, axis=1, keepdims=True)
    apq = jnp.sum(masked_first * second, axis=1, keepdims=True)
    tau = aqq - app
    square = tau * tau + 4.0 * apq * apq
    live = square > 0
    inverse = lax.rsqrt(jnp.where(live, square, 1.0))
    cos2 = 0.5 + 0.5 * jnp.abs(tau) * inverse
    root = lax.rsqrt(cos2)
    cosine = jnp.where(live, cos2 * root, 1.0)
    signed = jnp.where(tau >= 0, apq, -apq)
    sine = jnp.where(live, signed * inverse * root, 0.0)
    new_first = cosine * first - sine * second
    new_second = sine * first + cosine * second
    down = pltpu.roll(new_first, 1, 0)
    up = pltpu.roll(new_second, 7, 0)
    entering = pltpu.roll(new_second, 1, 0)
    top = jnp.where(sub == 0, new_first, jnp.where(sub == 1, entering, down))
    bottom = jnp.where(sub == 7, new_first, up)
    return top, bottom


def jacobi_start(upper):
    eye = (
        lax.broadcasted_iota(jnp.int32, (16, 16), 0) == lax.broadcasted_iota(jnp.int32, (16, 16), 1)
    ).astype(F32)
    both = jnp.concatenate([upper, eye], axis=1)
    return both[0:8], jnp.concatenate([both[i:i + 1] for i in range(15, 7, -1)], axis=0)


def spectrum(first, second, norm, ncell, upper, lower_inverse):
    both = jnp.concatenate([first, second], axis=0)
    scaled = both[:, 0:16]
    vecs = both[:, 16:32]
    lam = jnp.sum(scaled * scaled, axis=1, keepdims=True)
    row = lax.broadcasted_iota(jnp.int32, (16, 16), 0)
    col = lax.broadcasted_iota(jnp.int32, (16, 16), 1)
    along = jnp.sum(jnp.where(row == col, lam, 0.0), axis=0, keepdims=True)
    above = (along > lam).astype(F32)
    ties = ((along == lam) & (col < row)).astype(F32)
    greater = jnp.sum(above, axis=1, keepdims=True)
    keep = (greater < RANK - 0.5).astype(F32)
    place = greater + jnp.sum(ties, axis=1, keepdims=True)
    sigma = jnp.sqrt(lam * (norm / ncell))
    sigmas = jnp.sum(jnp.where(place == col.astype(F32), sigma, 0.0), axis=0, keepdims=True)
    proj = lax.dot_general(vecs * keep, vecs, TN, precision=HIGH, preferred_element_type=F32)
    weights = keep / (lam * norm)
    inverse = lax.dot_general(vecs * weights, vecs, TN, precision=HIGH, preferred_element_type=F32)
    before = jnp.dot(proj, lower_inverse, precision=HIGH, preferred_element_type=F32)
    after = lax.dot_general(upper, inverse, TN, precision=HIGH, preferred_element_type=F32)
    return before, after, sigmas


def slope_weights():
    base = np.zeros((132, 256), np.float32)
    for z in range(128):
        for step, lap, slope in ((-2, 0, 1), (-1, 1, -8), (0, -6, 0), (1, 1, 8), (2, 0, -1)):
            base[z + step + 2, z] += lap
            base[z + step + 2, 128 + z] += slope
    edge = base[[0, 1, 130, 131]]
    places = (np.arange(128) + 2) % 4
    return np.concatenate([base[2:130], base[2:130], edge[places]])


JACOBI_AT = 13


def step_kernel(
    sizes, ncell, snap, diff, slope, out, small,
    field, split, zbuf, ybuf, weights, yplo, yphi, zplo, zphi, ylo, yhi, zlo, zhi, mid, dbuf, obuf,
    gtotal, ctotal, state, factors, gslots, cslots,
    load_sem, aux_sem, out_sem, xs, xr, ys, yr, zs, zr, gs, gr, cs, cr,
):
    planes = dbuf.shape[0]
    parts = 4
    each = planes // parts

    def load(x, half):
        lanes = pl.ds(half * 128, 128)
        return pltpu.make_async_copy(
            snap.at[:, x, :, lanes], field.at[x + 2, :, half, pl.ds(8, 32)], load_sem.at[x, half]
        )

    for x in range(planes):
        for half in range(2):
            load(x, half).start()
    slope_copy = pltpu.make_async_copy(slope, weights, aux_sem.at[0])
    diff_copy = pltpu.make_async_copy(diff, dbuf, aux_sem.at[1])
    slope_copy.start()
    diff_copy.start()

    barrier = pltpu.get_barrier_semaphore()
    known = peers(sizes)
    for axis, target in known:
        pl.semaphore_signal(barrier, inc=1, device_id={axis: target}, device_id_type=MESH)
    near = {}
    for axis, count in zip(AXES, sizes):
        me = lax.axis_index(axis)
        near[axis] = (lax.rem(me + count - 1, count), lax.rem(me + 1, count))

    def remote(src, dst, send, recv, axis, side):
        return pltpu.make_async_remote_copy(
            src_ref=src, dst_ref=dst, send_sem=send, recv_sem=recv,
            device_id={axis: near[axis][side]}, device_id_type=MESH,
        )

    def x_copies():
        found = []
        for side in range(2):
            for p in range(2):
                for half in range(2):
                    source = p if side == 0 else planes - 2 + p
                    slot = planes + 2 + p if side == 0 else p
                    at = 4 * side + 2 * p + half
                    found.append(remote(
                        snap.at[:, source, :, pl.ds(half * 128, 128)],
                        field.at[slot, :, half, pl.ds(8, 32)],
                        xs.at[at], xr.at[at], "gx", side,
                    ))
        return found

    def yz_copies(part):
        span = pl.ds(part * each, each)
        a, b = 2 * part, 2 * part + 1
        return [
            remote(yplo.at[span], yhi.at[span], ys.at[a], yr.at[a], "gy", 0),
            remote(yphi.at[span], ylo.at[span], ys.at[b], yr.at[b], "gy", 1),
            remote(zplo.at[span], zhi.at[span], zs.at[a], zr.at[a], "gz", 0),
            remote(zphi.at[span], zlo.at[span], zs.at[b], zr.at[b], "gz", 1),
        ]

    lane = lax.broadcasted_iota(jnp.int32, (32, 128), 1)

    def pack(x, carry):
        for half in range(2):
            load(x, half).wait()
        left = jnp.zeros((32, 128), F32)
        right = jnp.zeros((32, 128), F32)
        centre = jnp.zeros((32, 128), F32)
        for k in range(SNAPS):
            for half in range(2):
                lanes = pl.ds(half * 128, 128)
                yplo[x, 2 * k:2 * k + 2, lanes] = field[x + 2, k, half, 8:10, :]
                yphi[x, 2 * k:2 * k + 2, lanes] = field[x + 2, k, half, 38:40, :]
            head = field[x + 2, k, 0, 8:40, :]
            tail = pltpu.roll(field[x + 2, k, 1, 8:40, :], (8 * k + 4) % 128, 1)
            if k:
                head = pltpu.roll(head, 8 * k, 1)
            left = jnp.where((lane >= 8 * k) & (lane < 8 * k + 2), head, left)
            right = jnp.where((lane >= 8 * k + 2) & (lane < 8 * k + 4), tail, right)
            centre = jnp.where((lane >= 8 * k + 4) & (lane < 8 * k + 6), tail, centre)
            low = (8 * k - 2) % 128
            centre = jnp.where((lane >= low) & (lane < low + 2), head, centre)
        zplo[x] = left
        zphi[x] = right
        mid[x] = centre
        for a in range(4):
            for half in range(2):
                high, low = halves(
                    field[x + 2, :, half, 8 + 8 * a:16 + 8 * a, :].reshape(128, 128)
                )
                split[x, a, 0:128, half * 128:half * 128 + 128] = high
                split[x, a, 128:256, half * 128:half * 128 + 128] = low
        both = jnp.concatenate([split[x, a] for a in range(4)], axis=1)
        gtotal[...] += lax.dot_general(both, both, NT, preferred_element_type=F32)
        return carry

    gtotal[...] = jnp.zeros_like(gtotal)
    ctotal[...] = jnp.zeros_like(ctotal)
    ybuf[...] = jnp.zeros_like(ybuf)
    for part in range(parts):
        lax.fori_loop(part * each, (part + 1) * each, pack, 0)
        if part == 0:
            pl.semaphore_wait(barrier, len(known))
            for copy in x_copies():
                copy.start()
        for copy in yz_copies(part):
            copy.start()
    sums = fold(gtotal[...], 2)
    mine = (sums[0:16, 0:16] + sums[16:32, 16:32]) + (sums[0:16, 16:32] + sums[16:32, 0:16])
    gram_args = (gslots, gs, gr)
    cross_args = (cslots, cs, cr)
    stage_start(sizes, 0, pack_square(mine), *gram_args)
    slope_copy.wait()
    diff_copy.wait()

    def write(x, slot):
        return pltpu.make_async_copy(obuf.at[slot], out.at[:, x], out_sem.at[slot])

    group = lax.broadcasted_iota(jnp.int32, (SNAPS, 8, 128), 0)
    own = (lax.broadcasted_iota(jnp.int32, (SNAPS, 8, 128), 2) + 2) % 128 // 8 == group

    def rotate(rounds):
        first, second = lax.fori_loop(
            0, rounds, lambda i, pair: jacobi_round(*pair), (state[0:8, 0:32], state[8:16, 0:32])
        )
        state[0:8, 0:32] = first
        state[8:16, 0:32] = second

    def cross(x):
        cat = functools.partial(jnp.concatenate, axis=1)
        ctotal[...] += lax.dot_general(
            cat([ybuf[a] for a in range(4)]), cat([split[x, a] for a in range(4)]),
            NT, preferred_element_type=F32,
        )

    def plane(i, carry):
        x = lax.rem(i + 2, planes)
        slot = lax.rem(i, 2)

        @pl.when(i == 0)
        def _():
            for copy in yz_copies(0):
                copy.wait()

        for part in range(1, parts):
            @pl.when(i == part * each - 2)
            def _(part=part):
                for copy in yz_copies(part):
                    copy.wait()

        @pl.when(i == planes - 4)
        def _():
            for copy in x_copies():
                copy.wait()

        @pl.when(i == JACOBI_AT - 5)
        def _():
            stage_start(sizes, 1, stage_finish(sizes, 0, *gram_args), *gram_args)

        @pl.when(i == JACOBI_AT - 2)
        def _():
            stage_start(sizes, 2, stage_finish(sizes, 1, *gram_args), *gram_args)

        @pl.when(i == JACOBI_AT)
        def _():
            upper, lower_inverse = factor(unpack_square(stage_finish(sizes, 2, *gram_args)))
            norm = jnp.sum(jnp.sum(upper * upper, axis=1, keepdims=True), axis=0, keepdims=True)
            first, second = jacobi_start(upper * lax.rsqrt(norm))
            state[0:8, 0:32] = first
            state[8:16, 0:32] = second
            factors[:, 0:16] = upper
            factors[:, 16:32] = lower_inverse

        @pl.when(i >= 2)
        def _():
            write(lax.rem(x + planes - 2, planes), slot).wait()

        cross(lax.rem(i + 1, planes))
        place = lane % 8
        outer = jnp.where(place < 2, zhi[x], jnp.where(place < 4, zlo[x], mid[x]))
        top = outer.astype(BF16).astype(F32)
        rest = outer - top
        inside = (place >= 2) & (place < 6)
        outer = [
            jnp.where(inside, top, pltpu.roll(rest, 124, 1)),
            jnp.where(inside, pltpu.roll(rest, 4, 1), top),
        ]
        rows = []
        for half in range(2):
            lanes = pl.ds(half * 128, 128)
            for a in range(4):
                edge = jnp.where(own, outer[half][8 * a:8 * a + 8, :][None], 0.0)
                rows.append(jnp.concatenate(
                    [
                        split[x, a, 0:128, lanes], split[x, a, 128:256, lanes],
                        edge.reshape(128, 128).astype(BF16),
                    ],
                    axis=1,
                ))
        zbuf[...] = jnp.dot(
            jnp.concatenate(rows, axis=0), weights[...], preferred_element_type=F32
        )
        for k in range(SNAPS):
            for half in range(2):
                lanes = pl.ds(half * 128, 128)
                field[x + 2, k, half, 6:8, :] = ylo[x, 2 * k:2 * k + 2, lanes]
                field[x + 2, k, half, 40:42, :] = yhi[x, 2 * k:2 * k + 2, lanes]

        def one(k, a, half):
            row = 8 + 8 * a
            at_z = pl.ds(pl.multiple_of(512 * half + 128 * a + 8 * k, 8), 8)

            def at(dx, dy):
                return field[x + 2 + dx, k, half, row + dy:row + dy + 8, :]

            lanes = pl.ds(half * 128, 128)
            u = at(0, 0)
            xp, xm, yp, ym = at(1, 0), at(-1, 0), at(0, 1), at(0, -1)
            lap = ((xp + xm) + (yp + ym)) + zbuf[at_z, 0:128]
            close = (xp - xm) + 0.75 * (yp - ym)
            far = (at(2, 0) - at(-2, 0)) + 0.75 * (at(0, 2) - at(0, -2))
            new = (u + dbuf[x, 8 * a:8 * a + 8, lanes] * lap) - (
                0.3 / 12.0 + (0.02 / 12.0) * u
            ) * zbuf[at_z, 128:256]
            new = new - ((1.6 / 12.0) * close - (0.2 / 12.0) * far)
            obuf[slot, k, 8 * a:8 * a + 8, lanes] = new
            return new

        def fields(j):
            k = 2 * j
            for a in range(4):
                for half in range(2):
                    lanes = pl.ds(half * 128, 128)
                    high, low = halves(
                        jnp.concatenate([one(k, a, half), one(k + 1, a, half)], axis=0)
                    )
                    ybuf[a, pl.ds(pl.multiple_of(8 * k, 16), 16), lanes] = high
                    ybuf[a, pl.ds(pl.multiple_of(128 + 8 * k, 16), 16), lanes] = low

        def plain(j, carry):
            fields(2 * j)
            fields(2 * j + 1)
            return carry

        def turning(j, pair):
            fields(j)
            return jacobi_round(*pair)

        @pl.when(i < JACOBI_AT)
        def _():
            lax.fori_loop(0, SNAPS // 4, plain, 0)

        @pl.when(i >= JACOBI_AT)
        def _():
            first, second = lax.fori_loop(
                0, SNAPS // 2, turning, (state[0:8, 0:32], state[8:16, 0:32])
            )
            state[0:8, 0:32] = first
            state[8:16, 0:32] = second

        write(x, slot).start()
        return carry

    lax.fori_loop(0, planes, plane, 0)
    cross(1)
    left_over = SWEEPS * 15 - (planes - JACOBI_AT) * (SNAPS // 2)
    sums = fold(ctotal[...], 2)
    turned = (sums[0:16, 0:16] + sums[0:16, 16:32]) + (sums[16:32, 0:16] + sums[16:32, 16:32])
    stage_start(sizes, 0, pack_square(turned), *cross_args)
    early, middle = left_over * 4 // 9, left_over // 3
    rotate(early)
    stage_start(sizes, 1, stage_finish(sizes, 0, *cross_args), *cross_args)
    rotate(middle)
    stage_start(sizes, 2, stage_finish(sizes, 1, *cross_args), *cross_args)
    rotate(left_over - early - middle)
    upper = factors[:, 0:16]
    norm = jnp.sum(jnp.sum(upper * upper, axis=1, keepdims=True), axis=0, keepdims=True)
    before, after, small[16:17, 0:16] = spectrum(
        state[0:8, 0:32], state[8:16, 0:32], norm, ncell, upper, factors[:, 16:32]
    )
    for slot in range(2):
        write(slot, slot).wait()
    turned = unpack_square(stage_finish(sizes, 2, *cross_args))
    middle = lax.dot_general(before, turned, NT, precision=HIGH, preferred_element_type=F32)
    small[0:16, 0:16] = jnp.dot(middle, after, precision=HIGH, preferred_element_type=F32)


def emit_kernel(held, small, out, reduced, sigmas, sem):
    copies = [
        pltpu.make_async_copy(held.at[k], out.at[k], sem.at[k]) for k in range(SNAPS)
    ]
    for copy in copies:
        copy.start()
    reduced[...] = small[0:16, 0:16]
    sigmas[...] = small[16:17, 0:16]
    for copy in copies:
        copy.wait()


def shards(sizes, snapshots, diffusivity):
    planes = snapshots.shape[1]
    ncell = float(planes * 32 * 256 * sizes[0] * sizes[1] * sizes[2])
    hbm = pl.BlockSpec(memory_space=pltpu.HBM)
    vmem = pl.BlockSpec(memory_space=pltpu.VMEM)
    links = sum(count - 1 for count in sizes)
    dma = pltpu.SemaphoreType.DMA
    shape = functools.partial(jax.ShapeDtypeStruct, dtype=F32)
    rows = [pltpu.VMEM((planes, 32, width), F32) for width in (256, 256, 128, 128)]
    held, small = pl.pallas_call(
        functools.partial(step_kernel, sizes, ncell),
        name="step",
        out_shape=[shape(snapshots.shape), shape((24, 128))],
        in_specs=[hbm] * 3,
        out_specs=[pl.BlockSpec(memory_space=pl.ANY), vmem],
        scratch_shapes=[
            pltpu.VMEM((planes + 4, SNAPS, 2, 48, 128), F32),
            pltpu.VMEM((planes, 4, 256, 256), BF16),
            pltpu.VMEM((1024, 256), F32),
            pltpu.VMEM((4, 256, 256), BF16),
            pltpu.VMEM((384, 256), BF16),
            *rows,
            *rows,
            pltpu.VMEM((planes, 32, 128), F32),
            pltpu.VMEM((planes, 32, 256), F32),
            pltpu.VMEM((2, SNAPS, 32, 256), F32),
            pltpu.VMEM((256, 256), F32), pltpu.VMEM((256, 256), F32),
            pltpu.VMEM((16, 128), F32), pltpu.VMEM((16, 128), F32),
            pltpu.VMEM((24, 8, 128), F32), pltpu.VMEM((24, 8, 128), F32),
            dma((planes, 2)), dma((2,)), dma((2,)),
            *[dma((8,))] * 6,
            *[dma((links,))] * 4,
        ],
        compiler_params=pltpu.CompilerParams(
            collective_id=0, has_side_effects=True, vmem_limit_bytes=42 << 20
        ),
    )(
        snapshots,
        pltpu.with_memory_space_constraint(diffusivity, pltpu.HBM),
        pltpu.with_memory_space_constraint(jnp.asarray(slope_weights(), BF16), pltpu.HBM),
    )
    shifted, reduced, sigmas = pl.pallas_call(
        emit_kernel,
        name="emit",
        out_shape=[shape(snapshots.shape), shape((16, 16)), shape((1, 16))],
        in_specs=[pl.BlockSpec(memory_space=pl.ANY), vmem],
        out_specs=[hbm, vmem, vmem],
        scratch_shapes=[dma((SNAPS,))],
        compiler_params=pltpu.CompilerParams(vmem_limit_bytes=4 << 20),
    )(held, small)
    return (shifted, reduced, sigmas.reshape(16))


def solution(mesh):
    sizes = tuple(mesh.shape[axis] for axis in AXES)
    return jax.shard_map(
        functools.partial(shards, sizes),
        mesh=mesh,
        in_specs=(P(None, "gx", "gy", "gz"), P("gx", "gy", "gz")),
        out_specs=(P(None, "gx", "gy", "gz"), P(), P()),
        check_vma=False,
    )
```
